256 devices in a mesh: front: 16 (over z, y_hi), row: 8 (over x, core), col: 2 (over y_lo).
Axes of the slice: x: 4, y: 4 (y_hi: 2, y_lo: 2; y = y_hi * 2 + y_lo), z: 8, core: 2. Of those that a mesh axis runs over, the one named last changes fastest.
Arguments:
- update_block: float32 [16, 4096, 4096], P('front', 'row', 'col'), may hold values from -6 to 6
- front_panel: float32 [16, 4096, 768], P('front', 'row', 'col'), may hold values from -6 to 6
- inverse_factor: float32 [16, 768, 768], P('front', None, 'col'), as said below
- child_tiles: bfloat16 [22016, 128, 128], P(('front', 'row', 'col')), may hold values from -6 to 6
- child_target: int32 [22016, 1], P(('front', 'row', 'col')), may hold values from 0 to 127; in each aligned block of 86 rows (0 to 85, 86 to 171, ...) at most 2 rows name the same one
- child_row: int32 [22016], P(('front', 'row', 'col')), may hold values from 0 to 3
- child_col: int32 [22016], P(('front', 'row', 'col')), may hold values from 0 to 15
- front_owner: int32 [16], replicated, may hold values from 0 to 15, each once
- live_tiles: int32 [16], P('front'), may hold values from 16 to 32
Outputs:
- schur: bfloat16 [16, 4096, 4096], P('front', 'row', 'col')
- panel: float32 [16, 4096, 768], P('front', 'row', 'col')
The draws below stay inside these ranges and needn't reach their ends.
Inputs may be any that keep to these rules, and one draw needn't show every extreme that they name: `inverse_factor`: lower triangular with a positive diagonal. `child_target`: in the rows of one device no value appears more than 2 times, and some value appears exactly 2 times. `front_owner`: each slot holds one front.
All inputs are finite; a program needn't handle non-finite values.
Results may differ from the reference program's by a relative error of at most 0.001.
Values may be sent and summed in bfloat16 or wider, within the bound.
A program may use at most 128 MiB of HBM per device.

```python
import math
import jax
import jax.numpy as jnp
import numpy as np
from jax import lax

U = 4096
P_SIZE = 768
TILE = 128
CAP = 2
FRONTS = 16
NT_DEV = 86
CHILDREN = 22016
ROW_TILES = 4
COL_TILES = 16
N_ROW = 8
N_COL = 2


def draw_inverse_factor(key, part):
    first, second = jax.random.split(key, 2)
    sigma = float(P_SIZE) ** (-0.75)
    entries = jax.random.normal(first, (FRONTS, P_SIZE, P_SIZE), jnp.float32)
    lower_part = jnp.tril(entries * sigma, -1)
    diagonal = jax.random.uniform(second, (FRONTS, P_SIZE), jnp.float32, 0.5, 1.5) * sigma * math.sqrt(float(P_SIZE))
    return (lower_part + diagonal[:, :, None] * jnp.eye(P_SIZE, dtype=jnp.float32)[None]).astype(jnp.float32)


def set_ends(values, rng, smallest, largest):
    shape = values.shape
    place = [jax.random.randint(jax.random.fold_in(rng, axis), (), 0, shape[axis]) for axis in range(len(shape))]
    values = values.at[tuple(place)].set(smallest)
    longest = shape.index(max(shape))
    place[longest] = (place[longest] + 1) % shape[longest]
    return values.at[tuple(place)].set(largest)


def levels(own_key, shape, cuts, smallest, largest):
    loudness = 1.0
    for axis_at, parts in cuts:
        draws = jax.random.uniform(jax.random.fold_in(jax.random.fold_in(own_key, 6), axis_at), (parts,), jnp.float32, smallest / len(cuts), largest / len(cuts))
        loudness = loudness * jnp.repeat(jnp.exp(draws), shape[axis_at] // parts).reshape((-1,) + (1,) * (len(shape) - 1 - axis_at))
    return loudness


def assign_block(own_key, own, number, rows, amount, top, most, skew):
    sequence = jax.random.permutation(own_key, amount)
    heavy_load, ordinary = shares(amount, rows * top, most, skew, True), shares(amount, rows * top, most, skew, False)
    places = jnp.arange(amount)

    def named(sizes, rotation):
        used = int((sizes > 0).sum())
        fixed = max(1, used // 4)
        passed = fixed + (places - fixed + rotation * (used - fixed)) % max(1, amount - fixed)
        return jnp.zeros((amount,), jnp.int32).at[sequence[jnp.where(places < fixed, places, passed)]].set(jnp.asarray(sizes, jnp.int32))

    sizes = jnp.where(number % 4 == 0, named(heavy_load, number // 4), named(ordinary, number - number // 4 - 1))
    mixed = jax.random.permutation(jax.random.fold_in(own, 3), amount)
    giver, sink = mixed[0:amount // 2 * 2:2], mixed[1:amount // 2 * 2:2]
    room = jnp.minimum(sizes[giver] - 1, most - sizes[sink]) // 2
    room = jnp.where((giver == sequence[0]) | (sink == sequence[0]) | (sizes[sink] == 0), 0, jnp.maximum(room, 0))
    passed = jax.random.randint(jax.random.fold_in(own, 4), (amount // 2,), 0, 1 << 20) % (room + 1)
    sizes = sizes.at[giver].add(-passed).at[sink].add(passed)
    members = jnp.searchsorted(jnp.cumsum(sizes), jnp.arange(rows * top), side="right").astype(jnp.int32)
    table = members.reshape(top, rows).T
    table = table[jax.random.permutation(jax.random.fold_in(own, 1), rows)]
    rotation = jax.random.randint(jax.random.fold_in(own, 2), (rows, 1), 0, top)
    return jnp.take_along_axis(table, (jnp.arange(top)[None, :] + rotation) % top, axis=1)


def shares(count, total, most, slope, full):
    weights = [(1 << 20) // math.isqrt(rank ** slope) + 1 for rank in range(1, count + 1)]
    largest = most if full else min(most, max(-(-total // count), total * weights[0] // sum(weights)))
    least = 1 if total - largest >= count - 1 else 0
    given, rest = [largest] + [least] * (count - 1), total - largest - least * (count - 1)
    while rest > 0:
        candidates = [i for i in range(1, count) if given[i] < largest] or [i for i in range(1, count) if given[i] < most]
        whole, budget = sum([weights[i] for i in candidates]), rest
        for i in candidates:
            more = min(most - given[i], max(1, budget * weights[i] // whole), rest)
            given[i] = given[i] + more
            rest = rest - more
    return np.array(given)


def normal_values(own_key, extent, deviation, limit, shards=(), kind=jnp.bfloat16):
    values = jax.random.normal(own_key, extent, jnp.float32) * deviation
    if len(shards) > 0:
        values = levels(own_key, extent, shards, -0.22, 0.18) * values
    return jnp.clip(values, min=-limit, max=limit).astype(kind)


def setup_inputs(seed: int = 0) -> dict:
    streams_of = jax.random.split(jax.random.key(seed), 10)
    update_block = normal_values(streams_of[0], (FRONTS, U, U), 1.0, 6.0, ((0, 16), (1, 8), (2, 2)), jnp.float32)
    front_panel = normal_values(streams_of[1], (FRONTS, U, P_SIZE), 1.0, 6.0, ((0, 16), (1, 8), (2, 2)), jnp.float32)
    inverse_factor = draw_inverse_factor(jax.random.fold_in(streams_of[9], 71), 0)
    child_tiles = normal_values(streams_of[3], (CHILDREN, TILE, TILE), 1.0, 6.0, ((0, 256),))
    child_target_keys = jax.random.split(jax.random.fold_in(streams_of[4], 1), CHILDREN // NT_DEV)
    child_target_turns = jax.random.permutation(jax.random.fold_in(streams_of[4], 3), CHILDREN // NT_DEV)
    child_target = jax.vmap(lambda own, number: assign_block(jax.random.fold_in(streams_of[4], 2), own, number, NT_DEV, FRONTS * N_ROW, 1, CAP, 2))(child_target_keys, child_target_turns).reshape((CHILDREN, 1))
    child_row = set_ends(jax.random.randint(streams_of[5], (CHILDREN,), 0, ROW_TILES), jax.random.fold_in(streams_of[5], 1), 0, ROW_TILES - 1).astype(jnp.int32)
    child_col = set_ends(jax.random.randint(streams_of[6], (CHILDREN,), 0, COL_TILES), jax.random.fold_in(streams_of[6], 1), 0, COL_TILES - 1).astype(jnp.int32)
    front_owner = jax.random.permutation(streams_of[7], FRONTS).astype(jnp.int32)
    live_tiles = set_ends(jax.random.randint(streams_of[8], (FRONTS,), U // TILE // 2, U // TILE + 1), jax.random.fold_in(streams_of[8], 1), U // TILE // 2, (U // TILE + 1) - 1).astype(jnp.int32)
    return {"update_block": update_block, "front_panel": front_panel, "inverse_factor": inverse_factor, "child_tiles": child_tiles, "child_target": child_target, "child_row": child_row, "child_col": child_col, "front_owner": front_owner, "live_tiles": live_tiles}


def reference(update_block, front_panel, inverse_factor, child_tiles, child_target, child_row, child_col, front_owner, live_tiles):
    highest = lax.Precision.HIGHEST
    live_bound = live_tiles.astype(jnp.int32) * TILE
    row_ids = jnp.arange(U, dtype=jnp.int32)
    factor_panel = jnp.einsum("fuk,fik->fui", front_panel, inverse_factor, precision=highest)
    factor_panel = jnp.where(row_ids[None, :, None] < live_bound[:, None, None], factor_panel, jnp.zeros_like(factor_panel))
    targets = child_target[:, 0].astype(jnp.int32)
    front_slot = front_owner.astype(jnp.int32)[targets // N_ROW]
    tile_row = (targets % N_ROW) * ROW_TILES + child_row.astype(jnp.int32)
    source_dev = jnp.arange(CHILDREN, dtype=jnp.int32) // NT_DEV
    tile_col = (source_dev % N_COL) * COL_TILES + child_col.astype(jnp.int32)
    grid_tiles = U // TILE
    child_values = child_tiles.astype(jnp.float32)
    assembled = jnp.zeros((FRONTS, grid_tiles, TILE, grid_tiles, TILE), jnp.float32)
    assembled = assembled.at[front_slot, tile_row, :, tile_col, :].add(child_values)
    assembled = assembled.reshape(FRONTS, U, U)

    def one_front(front_inputs):
        update_one, extra_one, panel_one, bound_one = front_inputs
        outer_part = jnp.dot(panel_one, panel_one.T, precision=highest, preferred_element_type=jnp.float32)
        updated = update_one + extra_one - outer_part
        inside = (row_ids[:, None] < bound_one) & (row_ids[None, :] < bound_one)
        return jnp.where(inside, updated, jnp.zeros_like(updated)).astype(jnp.bfloat16)

    schur = lax.map(one_front, (update_block, assembled, factor_panel, live_bound))
    return schur, factor_panel
```

```python
import functools

import jax
import jax.numpy as jnp
from jax import lax
from jax.experimental import pallas as pl
from jax.experimental.pallas import tpu as pltpu
from jax.sharding import PartitionSpec as P

TILE = 128
CAP = 2
MESH = pl.DeviceIdType.MESH


def pack_kernel(dests, rows_n, col_tiles, target, crow, ccol, owner, tiles, out, lab, count, sem):
    amount = tiles.shape[0]
    empty = 4 * col_tiles
    lab[...] = jnp.full(lab.shape, empty, jnp.int32)

    @pl.loop(0, dests)
    def _(i):
        count[i] = 0

    lane = lax.broadcasted_iota(jnp.int32, (1, 128), 1)

    @pl.loop(0, amount)
    def _(i):
        t = target[i]
        address = owner[t // rows_n] * rows_n + t % rows_n
        k = count[address]
        count[address] = k + 1
        pltpu.make_async_copy(tiles.at[i], out.at[k * dests + address], sem).start()
        place = crow[i] * col_tiles + ccol[i]
        lab[address] = jnp.where(lane == k, place, lab[address])

    pltpu.make_async_copy(tiles, out.at[pl.ds(0, amount)], sem).wait()


def peer_of(step, me, dests):
    return jnp.bitwise_xor(me, (step * 37) % dests)


def exchange_kernel(dests, rows_n, slot, with_lab, *refs):
    if with_lab:
        out, lab, inc, inclab, ssem, rsem, lsem, lssem, lrsem = refs
    else:
        out, inc, ssem, rsem, lsem = refs
    me = lax.axis_index("front") * rows_n + lax.axis_index("row")
    col = lax.axis_index("col")

    own = pltpu.make_async_copy(out.at[slot * dests + me], inc.at[me], lsem.at[0])
    own.start()
    if with_lab:
        ownlab = pltpu.make_async_copy(lab.at[me], inclab.at[me], lsem.at[1])
        ownlab.start()

    @pl.loop(1, dests)
    def _(step):
        p = peer_of(step, me, dests)
        dev = (p // rows_n, p % rows_n, col)
        pltpu.make_async_remote_copy(
            out.at[slot * dests + p], inc.at[me], ssem, rsem, device_id=dev, device_id_type=MESH
        ).start()
        if with_lab:
            pltpu.make_async_remote_copy(
                lab.at[p], inclab.at[me], lssem, lrsem, device_id=dev, device_id_type=MESH
            ).start()

    own.wait()
    some = pl.ds(0, dests - 1)
    both = pltpu.make_async_remote_copy(
        out.at[some], inc.at[some], ssem, rsem, device_id=(0, 0, 0), device_id_type=MESH
    )
    both.wait_send()
    both.wait_recv()
    if with_lab:
        ownlab.wait()
        labs = pltpu.make_async_remote_copy(
            lab.at[some], inclab.at[some], lssem, lrsem, device_id=(0, 0, 0), device_id_type=MESH
        )
        labs.wait_send()
        labs.wait_recv()


def assemble_kernel(group, col_tiles, lab, update, first, second, out):
    step = pl.program_id(0)
    empty = 4 * col_tiles

    @pl.when(step == 0)
    def _():
        out[...] = update[...]

    def add(place, tile):
        @pl.when(place < empty)
        def _():
            r = pl.multiple_of((place // col_tiles) * TILE, TILE)
            c = pl.multiple_of((place % col_tiles) * TILE, TILE)
            out[pl.ds(r, TILE), pl.ds(c, TILE)] += tile[...].astype(jnp.float32)

    @pl.loop(0, group)
    def _(j):
        add(lab[step * group + j, 0, 0], first.at[j])
        add(lab[step * group + j, 0, 1], second.at[j])


def per_device(
    update_block,
    front_panel,
    inverse_factor,
    child_tiles,
    child_target,
    child_row,
    child_col,
    front_owner,
    live_tiles,
):
    highest = lax.Precision.HIGHEST
    rows_dev = update_block.shape[1]
    cols_dev = update_block.shape[2]
    front_count = lax.axis_size("front")
    row_count = lax.axis_size("row")
    col_count = lax.axis_size("col")
    row_place = lax.axis_index("row")
    col_place = lax.axis_index("col")
    live_bound = live_tiles[0] * TILE
    row_ids = row_place * rows_dev + jnp.arange(rows_dev, dtype=jnp.int32)
    col_ids = col_place * cols_dev + jnp.arange(cols_dev, dtype=jnp.int32)
    dests = front_count * row_count
    col_tiles = cols_dev // TILE

    anyspace = pl.BlockSpec(memory_space=pl.ANY)
    smem = pl.BlockSpec(memory_space=pltpu.SMEM)
    tile_shape = (TILE, TILE)
    outgoing, labels = pl.pallas_call(
        functools.partial(pack_kernel, dests, row_count, col_tiles),
        out_shape=(
            jax.ShapeDtypeStruct((CAP * dests,) + tile_shape, jnp.bfloat16),
            jax.ShapeDtypeStruct((dests, 1, 128), jnp.int32),
        ),
        in_specs=[smem, smem, smem, smem, anyspace],
        out_specs=(anyspace, pl.BlockSpec(memory_space=pltpu.VMEM)),
        scratch_shapes=[pltpu.SMEM((dests,), jnp.int32), pltpu.SemaphoreType.DMA],
        name="pack",
    )(child_target[:, 0], child_row, child_col, front_owner, child_tiles)

    partial_value = lax.dot_general(
        front_panel[0],
        inverse_factor[0],
        (((1,), (1,)), ((), ())),
        precision=highest,
        preferred_element_type=jnp.float32,
    )
    partial_value = jnp.where(
        row_ids[:, None] < live_bound, partial_value, jnp.zeros_like(partial_value)
    )
    own_panel = lax.psum(partial_value, "col")

    inc_shape = jax.ShapeDtypeStruct((dests,) + tile_shape, jnp.bfloat16)
    dma = pltpu.SemaphoreType.DMA
    cost = pl.CostEstimate(flops=0, bytes_accessed=300_000_000, transcendentals=0)
    first, in_labels = pl.pallas_call(
        functools.partial(exchange_kernel, dests, row_count, 0, True),
        out_shape=(inc_shape, jax.ShapeDtypeStruct((dests, 1, 128), jnp.int32)),
        in_specs=[anyspace, anyspace],
        out_specs=(anyspace, anyspace),
        scratch_shapes=[dma, dma, dma((2,)), dma, dma],
        compiler_params=pltpu.CompilerParams(has_side_effects=True),
        cost_estimate=cost,
        name="exchange_a",
    )(outgoing, labels)
    outgoing, own_panel, first = lax.optimization_barrier((outgoing, own_panel, first))
    full_panel = lax.all_gather(own_panel, "row", axis=0, tiled=True)
    second = pl.pallas_call(
        functools.partial(exchange_kernel, dests, row_count, 1, False),
        out_shape=inc_shape,
        in_specs=[anyspace],
        out_specs=anyspace,
        scratch_shapes=[dma, dma, dma((2,))],
        compiler_params=pltpu.CompilerParams(has_side_effects=True),
        cost_estimate=cost,
        name="exchange_b",
    )(outgoing)

    group = 16
    with_children = pl.pallas_call(
        functools.partial(assemble_kernel, group, col_tiles),
        out_shape=jax.ShapeDtypeStruct((rows_dev, cols_dev), jnp.float32),
        grid=(dests // group,),
        in_specs=[
            smem,
            pl.BlockSpec((rows_dev, cols_dev), lambda i: (0, 0), pipeline_mode=pl.Buffered(1)),
            pl.BlockSpec((group,) + tile_shape, lambda i: (i, 0, 0)),
            pl.BlockSpec((group,) + tile_shape, lambda i: (i, 0, 0)),
        ],
        out_specs=pl.BlockSpec((rows_dev, cols_dev), lambda i: (0, 0)),
        compiler_params=pltpu.CompilerParams(vmem_limit_bytes=40 << 20),
        name="assemble",
    )(in_labels, update_block[0], first, second)

    columns = lax.dynamic_slice_in_dim(full_panel, col_place * cols_dev, cols_dev, 0)
    half_width = inverse_factor.shape[1] // col_count
    panel_out = lax.dynamic_slice_in_dim(own_panel, col_place * half_width, half_width, 1)[None]
    outer_part = lax.dot_general(
        own_panel,
        columns,
        (((1,), (1,)), ((), ())),
        precision=highest,
        preferred_element_type=jnp.float32,
    )
    updated = with_children - outer_part
    inside = (row_ids[:, None] < live_bound) & (col_ids[None, :] < live_bound)
    schur_out = jnp.where(inside, updated, jnp.zeros_like(updated)).astype(jnp.bfloat16)[None]
    return (schur_out, panel_out)


def solution(mesh):
    return jax.shard_map(
        per_device,
        mesh=mesh,
        in_specs=(
            P("front", "row", "col"),
            P("front", "row", "col"),
            P("front", None, "col"),
            P(("front", "row", "col"), None, None),
            P(("front", "row", "col"), None),
            P(("front", "row", "col")),
            P(("front", "row", "col")),
            P(),
            P("front"),
        ),
        out_specs=(P("front", "row", "col"), P("front", "row", "col")),
        check_vma=False,
    )
```

```python
import functools

import jax
import jax.numpy as jnp
from jax import lax
from jax.experimental import pallas as pl
from jax.experimental.pallas import tpu as pltpu
from jax.sharding import PartitionSpec as P

TILE = 128
FEW = 2
CHUNKS = 4
MESH = pl.DeviceIdType.MESH
DMA = pltpu.SemaphoreType.DMA


def index_kernel(fronts, rows_n, col_tiles, target, crow, ccol, owner, idx1, lab1, idx2, code2, idx3, lab3, over, count, few):
    dests = fronts * rows_n
    empty = 4 * col_tiles

    @pl.loop(0, dests)
    def _(i):
        count[i] = 0
        idx1[i] = 0
        idx3[i] = 0
        lab1[i, 0, 0] = empty
        lab3[i, 0, 0] = empty

    @pl.loop(0, fronts)
    def _(f):
        few[f] = 0
        for j in range(FEW):
            idx2[f * FEW + j] = 0
            code2[f, 0, j] = empty * rows_n

    over[0] = 0

    @pl.loop(0, target.shape[0])
    def _(i):
        t = target[i]
        front = owner[t // rows_n]
        row = t % rows_n
        address = front * rows_n + row
        place = crow[i] * col_tiles + ccol[i]
        seen = count[address]
        count[address] = seen + 1

        @pl.when(seen == 0)
        def _():
            idx1[address] = i
            lab1[address, 0, 0] = place

        @pl.when(seen > 0)
        def _():
            k = few[front]
            few[front] = k + 1

            @pl.when(k < FEW)
            def _():
                idx2[front * FEW + k] = i
                code2[front, 0, k] = row * empty + place

            @pl.when(k >= FEW)
            def _():
                idx3[address] = i
                lab3[address, 0, 0] = place
                over[0] = over[0] + 1


def spread_kernel(fronts, rows_n, idx2, code2, tiles, fown, in2, incode, fother, fcols,
                  send2, ts, tr, cs, cr, ys, yr, xs, xr, ks, kr):
    front, row, col = lax.axis_index("front"), lax.axis_index("row"), lax.axis_index("col")
    x, k = row // 2, row % 2
    j = (x + 4 - 2 * col) % 4
    step_rows = fown.shape[0] // CHUNKS

    def at_j(place):
        return (front, ((place + 2 * col) % 4) * 2 + k, col)

    mate = (front, x * 2 + 1 - k, col)
    across = (front, row, 1 - col)

    def part(i):
        return pl.ds(i * step_rows, step_rows)

    def remote(src, dst, ssem, rsem, dev):
        return pltpu.make_async_remote_copy(src, dst, ssem, rsem, device_id=dev, device_id_type=MESH)

    @pl.loop(0, CHUNKS)
    def _(i):
        remote(fown.at[part(i)], fother.at[part(i)], ys, yr.at[i], across).start()

    def give(which, half, i, src, dev):
        b = 2 * which + k
        remote(src, fcols.at[b, half, part(i)], xs, xr.at[which, half, i], dev).start()

    def to_mate(which, half, i, src):
        b = 2 * which + k
        remote(src, fcols.at[b, half, part(i)], ks, kr.at[which], mate).start()

    def own_out(half, i, src):
        @pl.when(j == 0)
        def _():
            give(0, half, i, src, at_j(3))
            give(0, half, i, src, at_j(1))
            to_mate(0, half, i, src)

        @pl.when(j == 1)
        def _():
            give(1, half, i, src, at_j(2))
            give(1, half, i, src, at_j(0))
            to_mate(1, half, i, src)

    @pl.loop(0, CHUNKS)
    def _(i):
        own_out(col, i, fown.at[part(i)])

    for t in range(FEW):
        in2[front * FEW + t] = tiles[idx2[front * FEW + t]]
    incode[front] = code2[front]

    @pl.loop(1, fronts)
    def _(s):
        f = jnp.bitwise_xor(front, (s * 7) % fronts)
        for t in range(FEW):
            send2[f * FEW + t] = tiles[idx2[f * FEW + t]]
        dev = (f, row, col)
        remote(send2.at[pl.ds(f * FEW, FEW)], in2.at[pl.ds(front * FEW, FEW)], ts, tr, dev).start()
        remote(code2.at[f], incode.at[front], cs, cr, dev).start()

    def arrived(which, half, i):
        b = 2 * which + k
        remote(fcols.at[b, half, part(i)], fcols.at[b, half, part(i)], xs, xr.at[which, half, i], mate).wait_recv()

    def pass_on(which, half, i, dev):
        b = 2 * which + k
        src = fcols.at[b, half, part(i)]
        if dev is not None:
            give(which, half, i, src, dev)
        to_mate(which, half, i, src)

    @pl.loop(0, 2 * CHUNKS + 1)
    def _(s):
        @pl.when(s < 2 * CHUNKS)
        def _():
            late = s // CHUNKS
            half = (col + late) % 2
            i = s % CHUNKS

            @pl.when(late == 1)
            def _():
                remote(fown.at[part(i)], fother.at[part(i)], ys, yr.at[i], across).wait_recv()
                own_out(half, i, fother.at[part(i)])

            @pl.when(j == 0)
            def _():
                arrived(1, half, i)
                pass_on(1, half, i, None)

            @pl.when(j == 1)
            def _():
                arrived(0, half, i)
                pass_on(0, half, i, None)

            @pl.when(j == 2)
            def _():
                arrived(1, half, i)
                pass_on(1, half, i, at_j(3))

            @pl.when(j == 3)
            def _():
                arrived(0, half, i)
                pass_on(0, half, i, at_j(2))

        @pl.when(s > 0)
        def _():
            half = (col + (s - 1) // CHUNKS) % 2
            i = (s - 1) % CHUNKS

            @pl.when(j == 2)
            def _():
                arrived(0, half, i)
                pass_on(0, half, i, None)

            @pl.when(j == 3)
            def _():
                arrived(1, half, i)
                pass_on(1, half, i, None)

    @pl.when(j < 2)
    def _():
        b = 2 * j + k
        fcols[b, col] = fown[...]
        fcols[b, 1 - col] = fother[...]

    remote(fown, fother, ys, yr.at[0], across).wait_send()
    pairs = fcols.at[pl.ds(0, 2)]
    remote(pairs, pairs, ks, kr.at[0], mate).wait_send()
    for which in range(2):
        b = 2 * which + 1 - k
        remote(fcols.at[b], fcols.at[b], ks, kr.at[which], mate).wait_recv()

    @pl.when(j < 2)
    def _():
        remote(pairs, pairs, xs, kr.at[0], mate).wait_send()

    @pl.when(j >= 2)
    def _():
        remote(fcols.at[0], fcols.at[0], xs, kr.at[0], mate).wait_send()

    some = pl.ds(0, (fronts - 1) * FEW)
    both = remote(send2.at[some], in2.at[some], ts, tr, mate)
    both.wait_send()
    both.wait_recv()
    most = pl.ds(0, fronts - 1)
    codes = remote(code2.at[most], incode.at[most], cs, cr, mate)
    codes.wait_send()
    codes.wait_recv()


def exchange_kernel(fronts, rows_n, hop, *refs):
    if hop:
        (idx, lab, tiles, code, codes_out, in2, inc, inlab, xin, xcodes,
         send, xsend, ssem, rsem, lssem, lrsem, xssem, xrsem, cssem, crsem, lsem) = refs
    else:
        idx, lab, tiles, inc, inlab, send, ssem, rsem, lssem, lrsem, lsem = refs
    dests = fronts * rows_n
    front, row, col = lax.axis_index("front"), lax.axis_index("row"), lax.axis_index("col")
    me = front * rows_n + row
    empty = 4 * 16

    def remote(src, dst, s, r, dev):
        return pltpu.make_async_remote_copy(src, dst, s, r, device_id=dev, device_id_type=MESH)

    def pack_row(r):
        @pl.loop(0, fronts)
        def _(g):
            t = jnp.where(code[g, 0, 1] // empty == r, 1, 0)
            xsend[r * fronts + g] = in2[g * FEW + t]

    send[me] = tiles[idx[me]]
    own = pltpu.make_async_copy(send.at[me], inc.at[me], lsem.at[0])
    own.start()
    ownlab = pltpu.make_async_copy(lab.at[me], inlab.at[me], lsem.at[1])
    ownlab.start()
    per = dests // rows_n

    @pl.loop(0, rows_n)
    def _(outer):
        @pl.loop(0, per)
        def _(inner):
            step = outer * per + inner

            @pl.when(step > 0)
            def _():
                p = jnp.bitwise_xor(me, (step * 37) % dests)
                dev = (p // rows_n, p % rows_n, col)
                send[p] = tiles[idx[p]]
                remote(send.at[p], inc.at[me], ssem, rsem, dev).start()
                remote(lab.at[p], inlab.at[me], lssem, lrsem, dev).start()

        if hop:
            @pl.when(outer > 0)
            def _():
                r = jnp.bitwise_xor(row, outer)
                pack_row(r)
                dev = (front, r, col)
                remote(xsend.at[pl.ds(r * fronts, fronts)], xin.at[pl.ds(row * fronts, fronts)], xssem, xrsem, dev).start()
                remote(codes_out, xcodes.at[row], cssem, crsem, dev).start()

    if hop:
        pack_row(row)
        mine = pl.ds(row * fronts, fronts)
        ownx = pltpu.make_async_copy(xsend.at[mine], xin.at[mine], lsem.at[2])
        ownx.start()
        ownc = pltpu.make_async_copy(codes_out, xcodes.at[row], lsem.at[3])
        ownc.start()
    own.wait()
    ownlab.wait()
    here = (front, row, col)
    some = pl.ds(0, dests - 1)
    both = remote(send.at[some], inc.at[some], ssem, rsem, here)
    both.wait_send()
    both.wait_recv()
    labs = remote(lab.at[some], inlab.at[some], lssem, lrsem, here)
    labs.wait_send()
    labs.wait_recv()
    if hop:
        ownx.wait()
        ownc.wait()
        some = pl.ds(0, (rows_n - 1) * fronts)
        xs = remote(xsend.at[some], xin.at[some], xssem, xrsem, here)
        xs.wait_send()
        xs.wait_recv()
        some = pl.ds(0, rows_n - 1)
        cs = remote(xcodes.at[some], xcodes.at[some], cssem, crsem, here)
        cs.wait_send()
        cs.wait_recv()


def add_tile(out, place, col_tiles, tile):
    @pl.when(place < 4 * col_tiles)
    def _():
        r = pl.multiple_of((place // col_tiles) * TILE, TILE)
        c = pl.multiple_of((place % col_tiles) * TILE, TILE)
        out[pl.ds(r, TILE), pl.ds(c, TILE)] += tile[...].astype(jnp.float32)


def more_kernel(group, col_tiles, lab, base, tiles, out):
    step = pl.program_id(0)

    @pl.when(step == 0)
    def _():
        out[...] = base[...]

    @pl.loop(0, group)
    def _(i):
        add_tile(out, lab[step * group + i, 0, 0], col_tiles, tiles.at[i])


def finish_kernel(group, col_tiles, steps, lab, code, live, base, first, second, out, total):
    step = pl.program_id(0)
    row, col = lax.axis_index("row"), lax.axis_index("col")
    empty = 4 * col_tiles

    @pl.when(step == 0)
    def _():
        total[...] = base[...]

    @pl.loop(0, group)
    def _(i):
        add_tile(total, lab[step * group + i, 0, 0], col_tiles, first.at[i])
        c0 = code[step, i, 0, 0]
        c1 = code[step, i, 0, 1]
        place = jnp.where(c1 // empty == row, c1 % empty, empty)
        place = jnp.where(c0 // empty == row, c0 % empty, place)
        add_tile(total, place, col_tiles, second.at[i])

    @pl.when(step == steps - 1)
    def _():
        bound = live[0] * TILE
        height, width = total.shape

        @pl.loop(0, height // TILE)
        def _(i):
            rows = pl.ds(pl.multiple_of(i * TILE, TILE), TILE)
            row_ids = row * height + i * TILE + lax.broadcasted_iota(jnp.int32, (TILE, width), 0)
            col_ids = col * width + lax.broadcasted_iota(jnp.int32, (TILE, width), 1)
            inside = (row_ids < bound) & (col_ids < bound)
            out[rows] = jnp.where(inside, total[rows], 0.0).astype(out.dtype)


def per_device(
    update_block,
    front_panel,
    inverse_factor,
    child_tiles,
    child_target,
    child_row,
    child_col,
    front_owner,
    live_tiles,
):
    highest = lax.Precision.HIGHEST
    rows_dev = update_block.shape[1]
    cols_dev = update_block.shape[2]
    fronts = lax.axis_size("front")
    rows_n = lax.axis_size("row")
    row_place = lax.axis_index("row")
    col_place = lax.axis_index("col")
    dests = fronts * rows_n
    col_tiles = cols_dev // TILE
    half = front_panel.shape[2]

    anyspace = pl.BlockSpec(memory_space=pl.ANY)
    smem = pl.BlockSpec(memory_space=pltpu.SMEM)
    vmem = pl.BlockSpec(memory_space=pltpu.VMEM)
    shape = jax.ShapeDtypeStruct
    tile_shape = (TILE, TILE)
    ints = lambda *s: shape(s, jnp.int32)
    params = pltpu.CompilerParams(has_side_effects=True, vmem_limit_bytes=40 << 20)

    idx1, lab1, idx2, code2, idx3, lab3, over = pl.pallas_call(
        functools.partial(index_kernel, fronts, rows_n, col_tiles),
        out_shape=(ints(dests), ints(dests, 1, 128), ints(fronts * FEW), ints(fronts, 1, 128),
                   ints(dests), ints(dests, 1, 128), ints(1)),
        in_specs=[smem] * 4,
        out_specs=(smem,) * 7,
        scratch_shapes=[pltpu.SMEM((dests,), jnp.int32), pltpu.SMEM((fronts,), jnp.int32)],
        name="index",
    )(child_target[:, 0], child_row, child_col, front_owner)

    factor = lax.all_gather(inverse_factor[0], "col", axis=1, tiled=True)
    over_all = lax.psum(over.astype(jnp.float32), ("front", "row", "col"))

    in2, incode, fother, fcols = pl.pallas_call(
        functools.partial(spread_kernel, fronts, rows_n),
        out_shape=(shape((fronts * FEW,) + tile_shape, jnp.bfloat16), ints(fronts, 1, 128),
                   shape((rows_dev, half), jnp.float32), shape((4, 2, rows_dev, half), jnp.float32)),
        in_specs=[smem, vmem, vmem, vmem],
        out_specs=(vmem,) * 4,
        scratch_shapes=[pltpu.VMEM((fronts * FEW,) + tile_shape, jnp.bfloat16)] + [DMA] * 5
        + [DMA((CHUNKS,)), DMA, DMA((2, 2, CHUNKS)), DMA, DMA((2,))],
        compiler_params=params,
        cost_estimate=pl.CostEstimate(flops=0, bytes_accessed=150_000_000, transcendentals=0),
        name="spread",
    )(idx2, code2, child_tiles, front_panel[0])

    inc_shape = shape((dests,) + tile_shape, jnp.bfloat16)
    send_buf = pltpu.VMEM((dests,) + tile_shape, jnp.bfloat16)
    first, in_labels, second, in_codes = pl.pallas_call(
        functools.partial(exchange_kernel, fronts, rows_n, True),
        out_shape=(inc_shape, ints(dests, 1, 128), inc_shape, ints(rows_n, fronts, 1, 128)),
        in_specs=[smem, anyspace, vmem, smem, anyspace, vmem],
        out_specs=(anyspace,) * 4,
        scratch_shapes=[send_buf, send_buf] + [DMA] * 8 + [DMA((4,))],
        compiler_params=params,
        cost_estimate=pl.CostEstimate(flops=0, bytes_accessed=300_000_000, transcendentals=0),
        name="exchange",
    )(idx1, lab1, child_tiles, incode, incode, in2)

    live_bound = live_tiles[0] * TILE
    row_ids = row_place * rows_dev + jnp.arange(rows_dev, dtype=jnp.int32)
    col_row_ids = col_place * cols_dev + jnp.arange(cols_dev, dtype=jnp.int32)

    def rows_of(left, right, ids):
        dims = (((1,), (1,)), ((), ()))
        value = lax.dot_general(left, factor[:, :half], dims, precision=highest, preferred_element_type=jnp.float32)
        value += lax.dot_general(right, factor[:, half:], dims, precision=highest, preferred_element_type=jnp.float32)
        return jnp.where(ids[:, None] < live_bound, value, jnp.zeros_like(value))

    mine = front_panel[0]
    swap = col_place == 1
    own_panel = rows_of(jnp.where(swap, fother, mine), jnp.where(swap, mine, fother), row_ids)
    columns = rows_of(fcols[:, 0].reshape(cols_dev, half), fcols[:, 1].reshape(cols_dev, half), col_row_ids)
    panel_out = lax.dynamic_slice_in_dim(own_panel, col_place * half, half, 1)[None]
    base = update_block[0] - lax.dot_general(
        own_panel, columns, (((1,), (1,)), ((), ())), precision=highest, preferred_element_type=jnp.float32
    )

    block = (rows_dev, cols_dev)
    group = dests // rows_n
    whole = pl.BlockSpec(block, lambda i: (0, 0), pipeline_mode=pl.Buffered(1))
    tiles_spec = pl.BlockSpec((group,) + tile_shape, lambda i: (i, 0, 0))

    def further(value):
        tiles3, labels3 = pl.pallas_call(
            functools.partial(exchange_kernel, fronts, rows_n, False),
            out_shape=(inc_shape, ints(dests, 1, 128)),
            in_specs=[smem, anyspace, vmem],
            out_specs=(anyspace,) * 2,
            scratch_shapes=[send_buf] + [DMA] * 4 + [DMA((4,))],
            compiler_params=params,
            name="further",
        )(idx3, lab3, child_tiles)
        return pl.pallas_call(
            functools.partial(more_kernel, group, col_tiles),
            out_shape=shape(block, jnp.float32),
            grid=(rows_n,),
            in_specs=[smem, whole, tiles_spec],
            out_specs=pl.BlockSpec(block, lambda i: (0, 0)),
            compiler_params=pltpu.CompilerParams(vmem_limit_bytes=40 << 20),
            name="more",
        )(labels3, value, tiles3)

    base = lax.cond(over_all[0] > 0, further, lambda value: value, base)

    schur_out = pl.pallas_call(
        functools.partial(finish_kernel, group, col_tiles, rows_n),
        out_shape=shape(block, jnp.bfloat16),
        grid=(rows_n,),
        in_specs=[smem, smem, smem, whole, tiles_spec, tiles_spec],
        out_specs=pl.BlockSpec(block, lambda i: (0, 0)),
        scratch_shapes=[pltpu.VMEM(block, jnp.float32)],
        compiler_params=pltpu.CompilerParams(vmem_limit_bytes=40 << 20),
        name="finish",
    )(in_labels, in_codes, live_tiles, base, first, second)[None]
    return (schur_out, panel_out)


def solution(mesh):
    return jax.shard_map(
        per_device,
        mesh=mesh,
        in_specs=(
            P("front", "row", "col"),
            P("front", "row", "col"),
            P("front", None, "col"),
            P(("front", "row", "col"), None, None),
            P(("front", "row", "col"), None),
            P(("front", "row", "col")),
            P(("front", "row", "col")),
            P(),
            P("front"),
        ),
        out_specs=(P("front", "row", "col"), P("front", "row", "col")),
        check_vma=False,
    )
```

```python
import functools

import jax
import jax.numpy as jnp
from jax import lax
from jax.experimental import pallas as pl
from jax.experimental.pallas import tpu as pltpu
from jax.sharding import PartitionSpec as P

TILE = 128
FEW = 3
CHUNKS = 4
MESH = pl.DeviceIdType.MESH
DMA = pltpu.SemaphoreType.DMA


def index_kernel(fronts, rows_n, col_tiles, target, crow, ccol, owner, idx1, lab1, idx2, code2, idx3, lab3, count, few, over):
    dests = fronts * rows_n
    empty = 4 * col_tiles

    @pl.loop(0, dests)
    def _(i):
        count[i] = 0
        idx1[i] = 0
        idx3[i] = 0
        lab1[i, 0, 0] = empty
        lab3[i, 0, 0] = empty

    @pl.loop(0, fronts)
    def _(f):
        few[f] = 0
        for j in range(FEW):
            idx2[f * FEW + j] = 0
            code2[f, 0, j] = empty * rows_n

    over[0] = 0

    @pl.loop(0, target.shape[0])
    def _(i):
        t = target[i]
        front = owner[t // rows_n]
        row = t % rows_n
        address = front * rows_n + row
        place = crow[i] * col_tiles + ccol[i]
        seen = count[address]
        count[address] = seen + 1

        @pl.when(seen == 0)
        def _():
            idx1[address] = i
            lab1[address, 0, 0] = place

        @pl.when(seen > 0)
        def _():
            k = few[front]
            few[front] = k + 1

            @pl.when(k < FEW)
            def _():
                idx2[front * FEW + k] = i
                code2[front, 0, k] = row * empty + place

            @pl.when(k >= FEW)
            def _():
                idx3[address] = i
                lab3[address, 0, 0] = place
                over[0] = over[0] + 1

    @pl.loop(0, fronts)
    def _(f):
        code2[f, 0, FEW] = over[0]


def spread_kernel(fronts, rows_n, idx2, code2, tiles, fown, in2, incode, fother, fcols,
                  send2, ts, tr, cs, cr, ys, yr, xs, xr, ks, kr):
    front, row, col = lax.axis_index("front"), lax.axis_index("row"), lax.axis_index("col")
    x, k = row // 2, row % 2
    j = (x + 4 - 2 * col) % 4
    step_rows = fown.shape[0] // CHUNKS

    def at_j(place):
        return (front, ((place + 2 * col) % 4) * 2 + k, col)

    mate = (front, x * 2 + 1 - k, col)
    across = (front, row, 1 - col)

    def part(i):
        return pl.ds(i * step_rows, step_rows)

    def remote(src, dst, ssem, rsem, dev):
        return pltpu.make_async_remote_copy(src, dst, ssem, rsem, device_id=dev, device_id_type=MESH)

    @pl.loop(0, CHUNKS)
    def _(i):
        remote(fown.at[part(i)], fother.at[part(i)], ys, yr.at[i], across).start()

    def give(which, half, i, src, dev):
        b = 2 * which + k
        remote(src, fcols.at[b, half, part(i)], xs, xr.at[which, half, i], dev).start()

    def to_mate(which, half, i, src):
        b = 2 * which + k
        remote(src, fcols.at[b, half, part(i)], ks, kr.at[which], mate).start()

    def own_out(half, i, src):
        @pl.when(j == 0)
        def _():
            give(0, half, i, src, at_j(3))
            give(0, half, i, src, at_j(1))
            to_mate(0, half, i, src)

        @pl.when(j == 1)
        def _():
            give(1, half, i, src, at_j(2))
            give(1, half, i, src, at_j(0))
            to_mate(1, half, i, src)

    @pl.loop(0, CHUNKS)
    def _(i):
        own_out(col, i, fown.at[part(i)])

    for t in range(FEW):
        in2[front * FEW + t] = tiles[idx2[front * FEW + t]]
    incode[front] = code2[front]

    @pl.loop(1, fronts)
    def _(s):
        f = jnp.bitwise_xor(front, (s * 7) % fronts)
        for t in range(FEW):
            send2[f * FEW + t] = tiles[idx2[f * FEW + t]]
        dev = (f, row, col)
        remote(send2.at[pl.ds(f * FEW, FEW)], in2.at[pl.ds(front * FEW, FEW)], ts, tr, dev).start()
        remote(code2.at[f], incode.at[front], cs, cr, dev).start()

    def arrived(which, half, i):
        b = 2 * which + k
        remote(fcols.at[b, half, part(i)], fcols.at[b, half, part(i)], xs, xr.at[which, half, i], mate).wait_recv()

    def pass_on(which, half, i, dev):
        b = 2 * which + k
        src = fcols.at[b, half, part(i)]
        if dev is not None:
            give(which, half, i, src, dev)
        to_mate(which, half, i, src)

    @pl.loop(0, 2 * CHUNKS + 1)
    def _(s):
        @pl.when(s < 2 * CHUNKS)
        def _():
            late = s // CHUNKS
            half = (col + late) % 2
            i = s % CHUNKS

            @pl.when(late == 1)
            def _():
                remote(fown.at[part(i)], fother.at[part(i)], ys, yr.at[i], across).wait_recv()
                own_out(half, i, fother.at[part(i)])

            @pl.when(j == 0)
            def _():
                arrived(1, half, i)
                pass_on(1, half, i, None)

            @pl.when(j == 1)
            def _():
                arrived(0, half, i)
                pass_on(0, half, i, None)

            @pl.when(j == 2)
            def _():
                arrived(1, half, i)
                pass_on(1, half, i, at_j(3))

            @pl.when(j == 3)
            def _():
                arrived(0, half, i)
                pass_on(0, half, i, at_j(2))

        @pl.when(s > 0)
        def _():
            half = (col + (s - 1) // CHUNKS) % 2
            i = (s - 1) % CHUNKS

            @pl.when(j == 2)
            def _():
                arrived(0, half, i)
                pass_on(0, half, i, None)

            @pl.when(j == 3)
            def _():
                arrived(1, half, i)
                pass_on(1, half, i, None)

    @pl.when(j < 2)
    def _():
        b = 2 * j + k
        fcols[b, col] = fown[...]
        fcols[b, 1 - col] = fother[...]

    remote(fown, fother, ys, yr.at[0], across).wait_send()
    pairs = fcols.at[pl.ds(0, 2)]
    remote(pairs, pairs, ks, kr.at[0], mate).wait_send()
    for which in range(2):
        b = 2 * which + 1 - k
        remote(fcols.at[b], fcols.at[b], ks, kr.at[which], mate).wait_recv()

    @pl.when(j < 2)
    def _():
        remote(pairs, pairs, xs, kr.at[0], mate).wait_send()

    @pl.when(j >= 2)
    def _():
        remote(fcols.at[0], fcols.at[0], xs, kr.at[0], mate).wait_send()

    some = pl.ds(0, (fronts - 1) * FEW)
    both = remote(send2.at[some], in2.at[some], ts, tr, mate)
    both.wait_send()
    both.wait_recv()
    most = pl.ds(0, fronts - 1)
    codes = remote(code2.at[most], incode.at[most], cs, cr, mate)
    codes.wait_send()
    codes.wait_recv()


def schur_base(live, fown, fother, fcols, factor, update, own_panel, base, panel):
    row, col = lax.axis_index("row"), lax.axis_index("col")
    height, width = base.shape
    half = fown.shape[1]
    step = height // 2
    bound = live[0] * TILE
    mine = pl.ds(pl.multiple_of(col * half, TILE), half)
    theirs = pl.ds(pl.multiple_of((1 - col) * half, TILE), half)

    def times(a, b):
        return lax.dot_general(
            a, b, (((1,), (1,)), ((), ())), precision=lax.Precision.HIGHEST, preferred_element_type=jnp.float32
        )

    def panel_rows(a, a_part, b, b_part, start):
        value = times(a, factor[:, a_part]) + times(b, factor[:, b_part])
        ids = start + lax.broadcasted_iota(jnp.int32, value.shape, 0)
        return jnp.where(ids < bound, value, 0.0)

    @pl.loop(0, 2)
    def _(i):
        rows = pl.ds(pl.multiple_of(i * step, step), step)
        own_panel[rows] = panel_rows(fown[rows], mine, fother[rows], theirs, row * height + i * step)

    panel[...] = own_panel[:, mine]

    @pl.loop(0, width // step)
    def _(c):
        rows = pl.ds(pl.multiple_of((c % 2) * step, step), step)
        value = panel_rows(
            fcols[c // 2, 0, rows], pl.ds(0, half), fcols[c // 2, 1, rows], pl.ds(half, half), col * width + c * step
        )
        lanes = pl.ds(pl.multiple_of(c * step, step), step)
        base[:, lanes] = update[:, lanes] - times(own_panel[...], value)


def exchange_kernel(fronts, rows_n, hop, *refs):
    if hop:
        (idx, lab, tiles, code, codes_out, in2, live, fown, fother, fcols, factor, update,
         inc, inlab, xin, xcodes, ycodes, over, base, panel,
         send, xsend, old, own_panel,
         ssem, rsem, lssem, lrsem, xssem, xrsem, cssem, crsem, yssem, yrsem, lsem) = refs
    else:
        idx, lab, tiles, inc, inlab, send, ssem, rsem, lssem, lrsem, lsem = refs
    dests = fronts * rows_n
    front, row, col = lax.axis_index("front"), lax.axis_index("row"), lax.axis_index("col")
    me = front * rows_n + row
    empty = 4 * 16

    def remote(src, dst, s, r, dev):
        return pltpu.make_async_remote_copy(src, dst, s, r, device_id=dev, device_id_type=MESH)

    def pack_row(r):
        @pl.loop(0, fronts)
        def _(g):
            t = 0
            for k in range(1, FEW):
                t = jnp.where(code[g, 0, k] // empty == r, k, t)
            xsend[r * fronts + g] = in2[g * FEW + t]

    if hop:
        fetch = pltpu.make_async_copy(update, old, lsem.at[4])
        fetch.start()
    send[me] = tiles[idx[me]]
    own = pltpu.make_async_copy(send.at[me], inc.at[me], lsem.at[0])
    own.start()
    ownlab = pltpu.make_async_copy(lab.at[me], inlab.at[me], lsem.at[1])
    ownlab.start()
    per = dests // rows_n

    @pl.loop(0, rows_n)
    def _(outer):
        @pl.loop(0, per)
        def _(inner):
            step = outer * per + inner

            @pl.when(step > 0)
            def _():
                p = jnp.bitwise_xor(me, (step * 37) % dests)
                dev = (p // rows_n, p % rows_n, col)
                send[p] = tiles[idx[p]]
                remote(send.at[p], inc.at[me], ssem, rsem, dev).start()
                remote(lab.at[p], inlab.at[me], lssem, lrsem, dev).start()

        if hop:
            @pl.when(outer > 0)
            def _():
                r = jnp.bitwise_xor(row, outer)
                pack_row(r)
                dev = (front, r, col)
                remote(xsend.at[pl.ds(r * fronts, fronts)], xin.at[pl.ds(row * fronts, fronts)], xssem, xrsem, dev).start()
                remote(codes_out, xcodes.at[row], cssem, crsem, dev).start()

            other = (front, jnp.bitwise_xor(row, outer), 1 - col)
            remote(codes_out, ycodes.at[row], yssem, yrsem, other).start()

    if hop:
        pack_row(row)
        mine = pl.ds(row * fronts, fronts)
        ownx = pltpu.make_async_copy(xsend.at[mine], xin.at[mine], lsem.at[2])
        ownx.start()
        ownc = pltpu.make_async_copy(codes_out, xcodes.at[row], lsem.at[3])
        ownc.start()
        fetch.wait()
        schur_base(live, fown, fother, fcols, factor, old, own_panel, base, panel)
    own.wait()
    ownlab.wait()
    here = (front, row, col)
    some = pl.ds(0, dests - 1)
    both = remote(send.at[some], inc.at[some], ssem, rsem, here)
    both.wait_send()
    both.wait_recv()
    labs = remote(lab.at[some], inlab.at[some], lssem, lrsem, here)
    labs.wait_send()
    labs.wait_recv()
    if hop:
        ownx.wait()
        ownc.wait()
        some = pl.ds(0, (rows_n - 1) * fronts)
        xs = remote(xsend.at[some], xin.at[some], xssem, xrsem, here)
        xs.wait_send()
        xs.wait_recv()
        some = pl.ds(0, rows_n - 1)
        cs = remote(xcodes.at[some], xcodes.at[some], cssem, crsem, here)
        cs.wait_send()
        cs.wait_recv()
        ys = remote(ycodes, ycodes, yssem, yrsem, here)
        ys.wait_send()
        ys.wait_recv()
        counts = jnp.sum(xcodes[...] + ycodes[...], axis=0)
        over[...] = jnp.sum(counts, axis=0)


def add_tile(out, place, col_tiles, tile):
    @pl.when(place < 4 * col_tiles)
    def _():
        r = pl.multiple_of((place // col_tiles) * TILE, TILE)
        c = pl.multiple_of((place % col_tiles) * TILE, TILE)
        out[pl.ds(r, TILE), pl.ds(c, TILE)] += tile[...].astype(jnp.float32)


def more_kernel(group, col_tiles, lab, base, tiles, out):
    step = pl.program_id(0)

    @pl.when(step == 0)
    def _():
        out[...] = base[...]

    @pl.loop(0, group)
    def _(i):
        add_tile(out, lab[step * group + i, 0, 0], col_tiles, tiles.at[i])


def finish_kernel(group, col_tiles, steps, lab, code, live, base, first, second, panel_in, out, panel_out, total):
    step = pl.program_id(0)
    row, col = lax.axis_index("row"), lax.axis_index("col")
    empty = 4 * col_tiles

    panel_out[...] = panel_in[...]

    @pl.when(step == 0)
    def _():
        total[...] = base[...]

    @pl.loop(0, group)
    def _(i):
        add_tile(total, lab[step * group + i, 0, 0], col_tiles, first.at[i])
        place = empty
        for k in range(FEW):
            c = code[step, i, 0, k]
            place = jnp.where(c // empty == row, c % empty, place)
        add_tile(total, place, col_tiles, second.at[i])

    @pl.when(step == steps - 1)
    def _():
        bound = live[0] * TILE
        height, width = total.shape

        @pl.loop(0, height // TILE)
        def _(i):
            rows = pl.ds(pl.multiple_of(i * TILE, TILE), TILE)
            row_ids = row * height + i * TILE + lax.broadcasted_iota(jnp.int32, (TILE, width), 0)
            col_ids = col * width + lax.broadcasted_iota(jnp.int32, (TILE, width), 1)
            inside = (row_ids < bound) & (col_ids < bound)
            out[rows] = jnp.where(inside, total[rows], 0.0).astype(out.dtype)


def per_device(
    update_block,
    front_panel,
    inverse_factor,
    child_tiles,
    child_target,
    child_row,
    child_col,
    front_owner,
    live_tiles,
):
    rows_dev = update_block.shape[1]
    cols_dev = update_block.shape[2]
    fronts = lax.axis_size("front")
    rows_n = lax.axis_size("row")
    dests = fronts * rows_n
    col_tiles = cols_dev // TILE
    half = front_panel.shape[2]

    anyspace = pl.BlockSpec(memory_space=pl.ANY)
    hbm = pl.BlockSpec(memory_space=pltpu.HBM)
    smem = pl.BlockSpec(memory_space=pltpu.SMEM)
    vmem = pl.BlockSpec(memory_space=pltpu.VMEM)
    shape = jax.ShapeDtypeStruct
    tile_shape = (TILE, TILE)
    ints = lambda *s: shape(s, jnp.int32)
    params = pltpu.CompilerParams(has_side_effects=True, vmem_limit_bytes=40 << 20)

    idx1, lab1, idx2, code2, idx3, lab3 = pl.pallas_call(
        functools.partial(index_kernel, fronts, rows_n, col_tiles),
        out_shape=(ints(dests), ints(dests, 1, 128), ints(fronts * FEW), ints(fronts, 1, 128),
                   ints(dests), ints(dests, 1, 128)),
        in_specs=[smem] * 4,
        out_specs=(smem,) * 6,
        scratch_shapes=[pltpu.SMEM((dests,), jnp.int32), pltpu.SMEM((fronts,), jnp.int32), pltpu.SMEM((1,), jnp.int32)],
        name="index",
    )(child_target[:, 0], child_row, child_col, front_owner)

    factor = lax.all_gather(inverse_factor[0], "col", axis=1, tiled=True)

    in2, incode, fother, fcols = pl.pallas_call(
        functools.partial(spread_kernel, fronts, rows_n),
        out_shape=(shape((fronts * FEW,) + tile_shape, jnp.bfloat16), ints(fronts, 1, 128),
                   shape((rows_dev, half), jnp.float32), shape((4, 2, rows_dev, half), jnp.float32)),
        in_specs=[smem, vmem, vmem, vmem],
        out_specs=(vmem,) * 4,
        scratch_shapes=[pltpu.VMEM((fronts * FEW,) + tile_shape, jnp.bfloat16)] + [DMA] * 5
        + [DMA((CHUNKS,)), DMA, DMA((2, 2, CHUNKS)), DMA, DMA((2,))],
        compiler_params=params,
        cost_estimate=pl.CostEstimate(flops=0, bytes_accessed=150_000_000, transcendentals=0),
        name="spread",
    )(idx2, code2, child_tiles, front_panel[0])

    block = (rows_dev, cols_dev)
    inc_shape = shape((dests,) + tile_shape, jnp.bfloat16)
    code_shape = ints(rows_n, fronts, 1, 128)
    send_buf = pltpu.VMEM((dests,) + tile_shape, jnp.bfloat16)
    first, in_labels, second, in_codes, _, over, base, panel_half = pl.pallas_call(
        functools.partial(exchange_kernel, fronts, rows_n, True),
        out_shape=(inc_shape, ints(dests, 1, 128), inc_shape, code_shape, code_shape, ints(1, 128),
                   shape(block, jnp.float32), shape((rows_dev, half), jnp.float32)),
        in_specs=[smem, anyspace, vmem, smem, anyspace, vmem, smem, vmem, vmem, vmem, vmem, anyspace],
        out_specs=(hbm, anyspace, hbm, vmem, vmem, vmem, vmem, vmem),
        scratch_shapes=[send_buf, send_buf, pltpu.VMEM(block, jnp.float32), pltpu.VMEM((rows_dev, 2 * half), jnp.float32)]
        + [DMA] * 10 + [DMA((5,))],
        compiler_params=pltpu.CompilerParams(has_side_effects=True, vmem_limit_bytes=46 << 20),
        cost_estimate=pl.CostEstimate(flops=0, bytes_accessed=300_000_000, transcendentals=0),
        name="exchange",
    )(idx1, lab1, child_tiles, incode, incode, in2, live_tiles, front_panel[0], fother, fcols, factor, update_block[0])

    group = dests // rows_n
    whole = pl.BlockSpec(block, lambda i: (0, 0), pipeline_mode=pl.Buffered(1))
    tiles_spec = pl.BlockSpec((group,) + tile_shape, lambda i: (i, 0, 0))

    def further(value):
        tiles3, labels3 = pl.pallas_call(
            functools.partial(exchange_kernel, fronts, rows_n, False),
            out_shape=(inc_shape, ints(dests, 1, 128)),
            in_specs=[smem, anyspace, vmem],
            out_specs=(anyspace,) * 2,
            scratch_shapes=[send_buf] + [DMA] * 4 + [DMA((4,))],
            compiler_params=params,
            name="further",
        )(idx3, lab3, child_tiles)
        return pl.pallas_call(
            functools.partial(more_kernel, group, col_tiles),
            out_shape=shape(block, jnp.float32),
            grid=(rows_n,),
            in_specs=[smem, whole, tiles_spec],
            out_specs=pl.BlockSpec(block, lambda i: (0, 0)),
            compiler_params=pltpu.CompilerParams(vmem_limit_bytes=40 << 20),
            name="more",
        )(labels3, value, tiles3)

    base = lax.cond(over[0, FEW] > 0, further, lambda value: value, base)

    panel_spec = pl.BlockSpec((rows_dev // rows_n, half), lambda i: (i, 0))
    schur_out, panel_out = pl.pallas_call(
        functools.partial(finish_kernel, group, col_tiles, rows_n),
        out_shape=(shape(block, jnp.bfloat16), shape((rows_dev, half), jnp.float32)),
        grid=(rows_n,),
        in_specs=[smem, smem, smem, whole, tiles_spec, tiles_spec, panel_spec],
        out_specs=(pl.BlockSpec(block, lambda i: (0, 0)), panel_spec),
        scratch_shapes=[pltpu.VMEM(block, jnp.float32)],
        compiler_params=pltpu.CompilerParams(vmem_limit_bytes=58 << 20),
        name="finish",
    )(in_labels, in_codes, live_tiles, base, first, second, panel_half)
    return (schur_out[None], panel_out[None])


def solution(mesh):
    return jax.shard_map(
        per_device,
        mesh=mesh,
        in_specs=(
            P("front", "row", "col"),
            P("front", "row", "col"),
            P("front", None, "col"),
            P(("front", "row", "col"), None, None),
            P(("front", "row", "col"), None),
            P(("front", "row", "col")),
            P(("front", "row", "col")),
            P(),
            P("front"),
        ),
        out_specs=(P("front", "row", "col"), P("front", "row", "col")),
        check_vma=False,
    )
```

```python
import functools

import jax
import jax.numpy as jnp
from jax import lax
from jax.experimental import pallas as pl
from jax.experimental.pallas import tpu as pltpu
from jax.sharding import PartitionSpec as P

TILE = 128
FEW = 3
CHUNKS = 4
MESH = pl.DeviceIdType.MESH
DMA = pltpu.SemaphoreType.DMA


def schur_base(live, fown, fother, fcols, wown, wother, update, own_panel, base, panel):
    row, col = lax.axis_index("row"), lax.axis_index("col")
    height, width = base.shape
    half = fown.shape[1]
    step = height // 2
    bound = live[0] * TILE
    mine = pl.ds(pl.multiple_of(col * half, TILE), half)

    def times(a, b):
        return lax.dot_general(
            a, b, (((1,), (1,)), ((), ())), precision=lax.Precision.HIGHEST, preferred_element_type=jnp.float32
        )

    def panel_rows(a, b, start):
        value = times(a, wown[...]) + times(b, wother[...])
        ids = start + lax.broadcasted_iota(jnp.int32, value.shape, 0)
        return jnp.where(ids < bound, value, 0.0)

    @pl.loop(0, 2)
    def _(i):
        rows = pl.ds(pl.multiple_of(i * step, step), step)
        own_panel[rows] = panel_rows(fown[rows], fother[rows], row * height + i * step)

    panel[...] = own_panel[:, mine]

    @pl.loop(0, width // step)
    def _(c):
        rows = pl.ds(pl.multiple_of((c % 2) * step, step), step)
        value = panel_rows(fcols[c // 2, col, rows], fcols[c // 2, 1 - col, rows], col * width + c * step)
        lanes = pl.ds(pl.multiple_of(c * step, step), step)
        base[:, lanes] = update[:, lanes] - times(own_panel[...], value)


def make_tables(fronts, rows_n, col_tiles, target, crow, ccol, owner, codes, picks, idx3, place3):
    dests = fronts * rows_n
    empty = 4 * col_tiles
    bits = rows_n.bit_length() - 1
    amount = target.shape[1]
    t = target[...]
    holder = jnp.zeros_like(t)
    for f in range(fronts):
        holder = jnp.where(lax.shift_right_arithmetic(t, bits) == f, owner[f], holder)
    address = holder * rows_n + (t & (rows_n - 1))
    place = crow[...] * col_tiles + ccol[...]
    grid = (dests, amount)
    i = lax.broadcasted_iota(jnp.int32, grid, 1)
    here = lax.broadcasted_iota(jnp.int32, grid, 0) == address
    wide = (fronts, rows_n, 128)

    def spread(column):
        return jnp.broadcast_to(column, (dests, 128)).reshape(wide)

    first = jnp.min(jnp.where(here, i, amount), axis=1, keepdims=True)
    last = jnp.max(jnp.where(here, i, -1), axis=1, keepdims=True)
    place1 = jnp.sum(jnp.where(i == first, place, 0), axis=1, keepdims=True)
    place2 = jnp.sum(jnp.where(i == last, place, 0), axis=1, keepdims=True)
    place1 = spread(jnp.where(first < amount, place1, empty))
    pick1 = spread(jnp.where(first < amount, first, 0))
    twice = spread(jnp.where(last > first, 1, 0))
    place2, last = spread(place2), spread(last)
    lane = lax.broadcasted_iota(jnp.int32, wide, 2)
    r = lax.broadcasted_iota(jnp.int32, wide, 1)
    rank = jnp.zeros(wide, jnp.int32)
    for q in range(rows_n - 1):
        rank = rank + jnp.where(r > q, twice[:, q : q + 1, :], 0)
    few = jnp.where((rank == lane) & (lane < FEW), twice, 0)
    firsts = lane - 8 == r
    left = jnp.where(rank >= FEW, twice, 0)

    def down(value):
        return jnp.sum(value, axis=1, keepdims=True)

    row_lane = lax.broadcasted_iota(jnp.int32, (fronts, 1, 128), 2)
    over = jnp.sum(down(left), axis=0, keepdims=True)
    code = down(few * (r * empty + place2)) + down(jnp.where(firsts, place1, 0))
    code = jnp.where((row_lane < FEW) & (down(few) == 0), rows_n * empty, code)
    codes[...] = jnp.where(row_lane == FEW, over, code)
    picks[...] = down(few * last) + down(jnp.where(firsts, pick1, 0))
    idx3[...] = (left * last).reshape(dests, 128)
    place3[...] = jnp.where(left > 0, place2, empty).reshape(dests, 128)


def remote(src, dst, ssem, rsem, dev):
    return pltpu.make_async_remote_copy(src, dst, ssem, rsem, device_id=dev, device_id_type=MESH)


def level_kernel(fronts, rows_n, col_tiles, target, crow, ccol, owner, live, tiles_hbm, fown, wown_hbm, update,
                 inc, xin, xcodes, ycodes, over, base, panel, idx3, place3,
                 tiles, send, xsend, send2, in2, codes, picks, incode, pick_s, code_s,
                 fownv, fother, fcols, wown, wother, old, own_panel,
                 ssem, rsem, xssem, xrsem, cssem, crsem, yssem, yrsem, ts, tr, cs, cr, ys, yr, xs, xr, ks, kr, ws, wr, wks, wkr, lsem):
    dests = fronts * rows_n
    empty = 4 * col_tiles
    front, row, col = lax.axis_index("front"), lax.axis_index("row"), lax.axis_index("col")
    me = front * rows_n + row
    x, k = row // 2, row % 2
    j = (x + 4 - 2 * col) % 4
    step_rows = fown.shape[0] // CHUNKS

    def at_j(place):
        return (front, ((place + 2 * col) % 4) * 2 + k, col)

    here = (front, row, col)
    mate = (front, x * 2 + 1 - k, col)
    across = (front, row, 1 - col)

    def part(i):
        return pl.ds(i * step_rows, step_rows)

    def load(n, src, dst):
        return pltpu.make_async_copy(src, dst, lsem.at[n])

    loads = [load(0, tiles_hbm, tiles), load(1, fown, fownv), load(2, wown_hbm, wown), load(3, update, old)]

    @pl.loop(0, CHUNKS)
    def _(i):
        remote(fown.at[part(i)], fother.at[part(i)], ys, yr.at[i], across).start()

    def give(which, half, i, src, dev):
        b = 2 * which + k
        remote(src, fcols.at[b, half, part(i)], xs, xr.at[which, half, i], dev).start()

    def to_mate(which, half, i, src):
        b = 2 * which + k
        remote(src, fcols.at[b, half, part(i)], ks, kr.at[which], mate).start()

    def own_out(half, i, src):
        @pl.when(j == 0)
        def _():
            give(0, half, i, src, at_j(3))
            give(0, half, i, src, at_j(1))
            to_mate(0, half, i, src)

        @pl.when(j == 1)
        def _():
            give(1, half, i, src, at_j(2))
            give(1, half, i, src, at_j(0))
            to_mate(1, half, i, src)

    @pl.loop(0, CHUNKS)
    def _(i):
        own_out(col, i, fown.at[part(i)])

    w_rows = wother.shape[0] // 2
    w_mine = pl.ds(pl.multiple_of(k * w_rows, TILE), w_rows)
    remote(wown_hbm.at[w_mine], wother.at[w_mine], ws, wr, across).start()
    for c in loads:
        c.start()

    make_tables(fronts, rows_n, col_tiles, target, crow, ccol, owner, codes, picks, idx3, place3)
    table = load(4, picks, pick_s)
    table.start()
    table.wait()
    loads[0].wait()

    for t in range(FEW):
        in2[front * FEW + t] = tiles[pick_s[front, 0, t]]
    incode[front] = codes[front]

    @pl.loop(1, fronts)
    def _(s):
        f = jnp.bitwise_xor(front, (s * 7) % fronts)
        for t in range(FEW):
            send2[f * FEW + t] = tiles[pick_s[f, 0, t]]
        dev = (f, row, col)
        remote(send2.at[pl.ds(f * FEW, FEW)], in2.at[pl.ds(front * FEW, FEW)], ts, tr, dev).start()
        remote(codes.at[f], incode.at[front], cs, cr, dev).start()

    send[me] = tiles[pick_s[front, 0, 8 + row]]
    own = load(5, send.at[me], inc.at[me])
    own.start()

    def arrived(which, half, i):
        b = 2 * which + k
        remote(fcols.at[b, half, part(i)], fcols.at[b, half, part(i)], xs, xr.at[which, half, i], mate).wait_recv()

    def pass_on(which, half, i, dev):
        b = 2 * which + k
        src = fcols.at[b, half, part(i)]
        if dev is not None:
            give(which, half, i, src, dev)
        to_mate(which, half, i, src)

    per = dests // (2 * CHUNKS)

    @pl.loop(0, 2 * CHUNKS + 1)
    def _(s):
        @pl.when(s < 2 * CHUNKS)
        def _():
            @pl.loop(0, per)
            def _(inner):
                n = s * per + inner

                @pl.when(n > 0)
                def _():
                    p = jnp.bitwise_xor(me, (n * 37) % dests)
                    f, r = p // rows_n, p % rows_n
                    send[p] = tiles[pick_s[f, 0, 8 + r]]
                    remote(send.at[p], inc.at[me], ssem, rsem, (f, r, col)).start()

            late = s // CHUNKS
            half = (col + late) % 2
            i = s % CHUNKS

            @pl.when(late == 1)
            def _():
                remote(fown.at[part(i)], fother.at[part(i)], ys, yr.at[i], across).wait_recv()
                own_out(half, i, fother.at[part(i)])

            @pl.when(s == CHUNKS)
            def _():
                whalf = remote(wother.at[w_mine], wother.at[w_mine], wks, wr, mate)
                whalf.wait_recv()
                remote(wother.at[w_mine], wother.at[w_mine], wks, wkr, mate).start()

            @pl.when(j == 0)
            def _():
                arrived(1, half, i)
                pass_on(1, half, i, None)

            @pl.when(j == 1)
            def _():
                arrived(0, half, i)
                pass_on(0, half, i, None)

            @pl.when(j == 2)
            def _():
                arrived(1, half, i)
                pass_on(1, half, i, at_j(3))

            @pl.when(j == 3)
            def _():
                arrived(0, half, i)
                pass_on(0, half, i, at_j(2))

        @pl.when(s > 0)
        def _():
            half = (col + (s - 1) // CHUNKS) % 2
            i = (s - 1) % CHUNKS

            @pl.when(j == 2)
            def _():
                arrived(0, half, i)
                pass_on(0, half, i, None)

            @pl.when(j == 3)
            def _():
                arrived(1, half, i)
                pass_on(1, half, i, None)

    some = pl.ds(0, (fronts - 1) * FEW)
    both = remote(send2.at[some], in2.at[some], ts, tr, mate)
    both.wait_send()
    both.wait_recv()
    most = pl.ds(0, fronts - 1)
    got = remote(codes.at[most], incode.at[most], cs, cr, mate)
    got.wait_send()
    got.wait_recv()
    table = load(4, incode, code_s)
    table.start()
    table.wait()

    def pack_row(r):
        @pl.loop(0, fronts)
        def _(g):
            t = 0
            for q in range(1, FEW):
                t = jnp.where(code_s[g, 0, q] // empty == r, q, t)
            xsend[r * fronts + g] = in2[g * FEW + t]

    @pl.loop(0, rows_n)
    def _(s):
        r = jnp.bitwise_xor(row, s)

        @pl.when(s > 0)
        def _():
            pack_row(r)
            dev = (front, r, col)
            remote(xsend.at[pl.ds(r * fronts, fronts)], xin.at[pl.ds(row * fronts, fronts)], xssem, xrsem, dev).start()
            remote(incode, xcodes.at[row], cssem, crsem, dev).start()

        remote(incode, ycodes.at[row], yssem, yrsem, (front, r, 1 - col)).start()

    pack_row(row)
    mine = pl.ds(row * fronts, fronts)
    ownx = load(4, xsend.at[mine], xin.at[mine])
    ownx.start()
    xcodes[row] = incode[...]

    for which in range(2):
        b = 2 * which + 1 - k
        remote(fcols.at[b], fcols.at[b], ks, kr.at[which], mate).wait_recv()
    w_other = pl.ds(pl.multiple_of((1 - k) * w_rows, TILE), w_rows)
    remote(wother.at[w_other], wother.at[w_other], wks, wkr, mate).wait_recv()
    for c in loads[1:]:
        c.wait()

    @pl.when(j < 2)
    def _():
        b = 2 * j + k
        fcols[b, col] = fownv[...]
        fcols[b, 1 - col] = fother[...]

    schur_base(live, fownv, fother, fcols, wown, wother, old, own_panel, base, panel)

    remote(fown, fother, ys, yr.at[0], across).wait_send()
    remote(wother.at[w_mine], wother.at[w_mine], ws, wr, across).wait_send()
    remote(wother.at[w_mine], wother.at[w_mine], wks, wkr, mate).wait_send()
    pairs = fcols.at[pl.ds(0, 2)]
    remote(pairs, pairs, ks, kr.at[0], mate).wait_send()

    @pl.when(j < 2)
    def _():
        remote(pairs, pairs, xs, kr.at[0], mate).wait_send()

    @pl.when(j >= 2)
    def _():
        remote(fcols.at[0], fcols.at[0], xs, kr.at[0], mate).wait_send()

    own.wait()
    ownx.wait()
    some = pl.ds(0, dests - 1)
    both = remote(send.at[some], inc.at[some], ssem, rsem, here)
    both.wait_send()
    both.wait_recv()
    some = pl.ds(0, (rows_n - 1) * fronts)
    both = remote(xsend.at[some], xin.at[some], xssem, xrsem, here)
    both.wait_send()
    both.wait_recv()
    some = pl.ds(0, rows_n - 1)
    both = remote(xcodes.at[some], xcodes.at[some], cssem, crsem, here)
    both.wait_send()
    both.wait_recv()
    both = remote(ycodes, ycodes, yssem, yrsem, here)
    both.wait_send()
    both.wait_recv()
    counts = jnp.sum(xcodes[...] + ycodes[...], axis=0)
    over[...] = jnp.sum(counts, axis=0)


def further_kernel(fronts, rows_n, idx, lab, tiles, inc, inlab, send, ssem, rsem, lssem, lrsem, lsem):
    dests = fronts * rows_n
    front, row, col = lax.axis_index("front"), lax.axis_index("row"), lax.axis_index("col")
    me = front * rows_n + row
    send[me] = tiles[idx[me]]
    own = pltpu.make_async_copy(send.at[me], inc.at[me], lsem.at[0])
    own.start()
    ownlab = pltpu.make_async_copy(lab.at[me], inlab.at[me], lsem.at[1])
    ownlab.start()

    @pl.loop(1, dests)
    def _(n):
        p = jnp.bitwise_xor(me, (n * 37) % dests)
        dev = (p // rows_n, p % rows_n, col)
        send[p] = tiles[idx[p]]
        remote(send.at[p], inc.at[me], ssem, rsem, dev).start()
        remote(lab.at[p], inlab.at[me], lssem, lrsem, dev).start()

    own.wait()
    ownlab.wait()
    some = pl.ds(0, dests - 1)
    both = remote(send.at[some], inc.at[some], ssem, rsem, (front, row, col))
    both.wait_send()
    both.wait_recv()
    labs = remote(lab.at[some], inlab.at[some], lssem, lrsem, (front, row, col))
    labs.wait_send()
    labs.wait_recv()


def add_tile(out, place, col_tiles, tile):
    @pl.when(place < 4 * col_tiles)
    def _():
        r = pl.multiple_of((place // col_tiles) * TILE, TILE)
        c = pl.multiple_of((place % col_tiles) * TILE, TILE)
        out[pl.ds(r, TILE), pl.ds(c, TILE)] += tile[...].astype(jnp.float32)


def more_kernel(group, col_tiles, lab, base, tiles, out):
    step = pl.program_id(0)

    @pl.when(step == 0)
    def _():
        out[...] = base[...]

    @pl.loop(0, group)
    def _(i):
        add_tile(out, lab[step * group + i, 0, 0], col_tiles, tiles.at[i])


def finish_kernel(group, col_tiles, steps, rows_n, code, live, base, first, second, panel_in, out, panel_out, total):
    step = pl.program_id(0)
    row, col = lax.axis_index("row"), lax.axis_index("col")
    empty = 4 * col_tiles

    panel_out[...] = panel_in[...]

    @pl.when(step == 0)
    def _():
        total[...] = base[...]

    @pl.loop(0, group)
    def _(i):
        source = step * group + i
        place = code[source % rows_n, source // rows_n, 0, 8 + row]
        add_tile(total, place, col_tiles, first.at[i])
        place = empty
        for k in range(FEW):
            c = code[step, i, 0, k]
            place = jnp.where(c // empty == row, c % empty, place)
        add_tile(total, place, col_tiles, second.at[i])

    @pl.when(step == steps - 1)
    def _():
        bound = live[0] * TILE
        height, width = total.shape

        @pl.loop(0, height // TILE)
        def _(i):
            rows = pl.ds(pl.multiple_of(i * TILE, TILE), TILE)
            row_ids = row * height + i * TILE + lax.broadcasted_iota(jnp.int32, (TILE, width), 0)
            col_ids = col * width + lax.broadcasted_iota(jnp.int32, (TILE, width), 1)
            inside = (row_ids < bound) & (col_ids < bound)
            out[rows] = jnp.where(inside, total[rows], 0.0).astype(out.dtype)


def per_device(
    update_block,
    front_panel,
    inverse_factor,
    child_tiles,
    child_target,
    child_row,
    child_col,
    front_owner,
    live_tiles,
):
    rows_dev = update_block.shape[1]
    cols_dev = update_block.shape[2]
    fronts = lax.axis_size("front")
    rows_n = lax.axis_size("row")
    dests = fronts * rows_n
    col_tiles = cols_dev // TILE
    half = front_panel.shape[2]

    anyspace = pl.BlockSpec(memory_space=pl.ANY)
    hbm = pl.BlockSpec(memory_space=pltpu.HBM)
    smem = pl.BlockSpec(memory_space=pltpu.SMEM)
    vmem = pl.BlockSpec(memory_space=pltpu.VMEM)
    shape = jax.ShapeDtypeStruct
    tile_shape = (TILE, TILE)
    ints = lambda *s: shape(s, jnp.int32)
    params = pltpu.CompilerParams(has_side_effects=True, vmem_limit_bytes=40 << 20)

    block = (rows_dev, cols_dev)
    group = dests // rows_n
    inc_shape = shape((dests,) + tile_shape, jnp.bfloat16)
    code_shape = ints(rows_n, fronts, 1, 128)
    rows_buf = lambda *n: pltpu.VMEM(n + (rows_dev, half), jnp.float32)
    tiles_buf = lambda n: pltpu.VMEM((n,) + tile_shape, jnp.bfloat16)
    table = lambda space: space((fronts, 1, 128), jnp.int32)
    amount = child_tiles.shape[0]
    first, second, in_codes, _, over, base, panel_half, idx3, place3 = pl.pallas_call(
        functools.partial(level_kernel, fronts, rows_n, col_tiles),
        out_shape=(inc_shape, inc_shape, code_shape, code_shape, ints(1, 128), shape(block, jnp.float32),
                   shape((rows_dev, half), jnp.float32), ints(dests, 128), ints(dests, 128)),
        in_specs=[vmem, vmem, vmem, smem, smem, anyspace, anyspace, anyspace, anyspace],
        out_specs=(hbm, hbm) + (vmem,) * 7,
        scratch_shapes=[
            tiles_buf(amount), tiles_buf(dests), tiles_buf(dests), tiles_buf(fronts * FEW), tiles_buf(fronts * FEW),
            table(pltpu.VMEM), table(pltpu.VMEM), table(pltpu.VMEM), table(pltpu.SMEM), table(pltpu.SMEM),
            rows_buf(), rows_buf(), rows_buf(4, 2),
            pltpu.VMEM((2 * half, half), jnp.float32), pltpu.VMEM((2 * half, half), jnp.float32),
            pltpu.VMEM(block, jnp.float32), pltpu.VMEM((rows_dev, 2 * half), jnp.float32),
        ] + [DMA] * 13 + [DMA((CHUNKS,)), DMA, DMA((2, 2, CHUNKS)), DMA, DMA((2,))] + [DMA] * 4 + [DMA((6,))],
        compiler_params=pltpu.CompilerParams(has_side_effects=True, vmem_limit_bytes=58 << 20),
        cost_estimate=pl.CostEstimate(flops=0, bytes_accessed=300_000_000, transcendentals=0),
        name="level",
    )(child_target.reshape(1, amount), child_row.reshape(1, amount), child_col.reshape(1, amount), front_owner, live_tiles,
      child_tiles, front_panel[0], inverse_factor[0], update_block[0])

    whole = pl.BlockSpec(block, lambda i: (0, 0), pipeline_mode=pl.Buffered(1))
    tiles_spec = pl.BlockSpec((group,) + tile_shape, lambda i: (i, 0, 0))

    def further(value):
        labels = jnp.broadcast_to(place3[:, :1, None], (dests, 1, 128))
        tiles3, labels3 = pl.pallas_call(
            functools.partial(further_kernel, fronts, rows_n),
            out_shape=(inc_shape, ints(dests, 1, 128)),
            in_specs=[smem, anyspace, vmem],
            out_specs=(anyspace,) * 2,
            scratch_shapes=[tiles_buf(dests)] + [DMA] * 4 + [DMA((2,))],
            compiler_params=params,
            name="further",
        )(idx3[:, 0], labels, child_tiles)
        return pl.pallas_call(
            functools.partial(more_kernel, group, col_tiles),
            out_shape=shape(block, jnp.float32),
            grid=(rows_n,),
            in_specs=[smem, whole, tiles_spec],
            out_specs=pl.BlockSpec(block, lambda i: (0, 0)),
            compiler_params=pltpu.CompilerParams(vmem_limit_bytes=40 << 20),
            name="more",
        )(labels3, value, tiles3)

    base = lax.cond(over[0, FEW] > 0, further, lambda value: value, base)

    panel_spec = pl.BlockSpec((rows_dev // rows_n, half), lambda i: (i, 0))
    schur_out, panel_out = pl.pallas_call(
        functools.partial(finish_kernel, group, col_tiles, rows_n, rows_n),
        out_shape=(shape(block, jnp.bfloat16), shape((rows_dev, half), jnp.float32)),
        grid=(rows_n,),
        in_specs=[smem, smem, whole, tiles_spec, tiles_spec, panel_spec],
        out_specs=(pl.BlockSpec(block, lambda i: (0, 0)), panel_spec),
        scratch_shapes=[pltpu.VMEM(block, jnp.float32)],
        compiler_params=pltpu.CompilerParams(vmem_limit_bytes=58 << 20),
        name="finish",
    )(in_codes, live_tiles, base, first, second, panel_half)
    return (schur_out[None], panel_out[None])


def solution(mesh):
    return jax.shard_map(
        per_device,
        mesh=mesh,
        in_specs=(
            P("front", "row", "col"),
            P("front", "row", "col"),
            P("front", None, "col"),
            P(("front", "row", "col"), None, None),
            P(("front", "row", "col"), None),
            P(("front", "row", "col")),
            P(("front", "row", "col")),
            P(),
            P("front"),
        ),
        out_specs=(P("front", "row", "col"), P("front", "row", "col")),
        check_vma=False,
    )
```

```python
import functools

import jax
import jax.numpy as jnp
from jax import lax
from jax.experimental import pallas as pl
from jax.experimental.pallas import tpu as pltpu
from jax.sharding import PartitionSpec as P

TILE = 128
FEW = 3
EARLY = 72
CHUNKS = 2
MESH = pl.DeviceIdType.MESH
DMA = pltpu.SemaphoreType.DMA


def schur_base(live, fown, fother, fcols, wown, wother, update, own_panel, panel):
    row, col = lax.axis_index("row"), lax.axis_index("col")
    height, width = update.shape
    half = fown.shape[1]
    step = height // 2
    bound = live[0] * TILE
    mine = pl.ds(pl.multiple_of(col * half, TILE), half)

    def times(a, b):
        return lax.dot_general(
            a, b, (((1,), (1,)), ((), ())), precision=lax.Precision.HIGHEST, preferred_element_type=jnp.float32
        )

    def panel_rows(a, b, start):
        value = times(a, wown[...]) + times(b, wother[...])
        ids = start + lax.broadcasted_iota(jnp.int32, value.shape, 0)
        return jnp.where(ids < bound, value, 0.0)

    @pl.loop(0, 2)
    def _(i):
        rows = pl.ds(pl.multiple_of(i * step, step), step)
        own_panel[rows] = panel_rows(fown[rows], fother[rows], row * height + i * step)

    panel[...] = own_panel[:, mine]

    @pl.loop(0, width // step)
    def _(c):
        rows = pl.ds(pl.multiple_of((c % 2) * step, step), step)
        value = panel_rows(fcols[c // 2, col, rows], fcols[c // 2, 1 - col, rows], col * width + c * step)
        lanes = pl.ds(pl.multiple_of(c * step, step), step)
        update[:, lanes] = update[:, lanes] - times(own_panel[...], value)


def make_tables(fronts, rows_n, col_tiles, target, crow, ccol, owner, codes, picks, idx3, place3):
    dests = fronts * rows_n
    empty = 4 * col_tiles
    bits = rows_n.bit_length() - 1
    amount = target.shape[1]
    t = target[...]
    holder = jnp.zeros_like(t)
    for f in range(fronts):
        holder = jnp.where(lax.shift_right_arithmetic(t, bits) == f, owner[f], holder)
    address = holder * rows_n + (t & (rows_n - 1))
    place = crow[...] * col_tiles + ccol[...]
    grid = (dests, amount)
    i = lax.broadcasted_iota(jnp.int32, grid, 1)
    here = lax.broadcasted_iota(jnp.int32, grid, 0) == address
    wide = (fronts, rows_n, 128)

    def spread(column):
        return jnp.broadcast_to(column, (dests, 128)).reshape(wide)

    first = jnp.min(jnp.where(here, i, amount), axis=1, keepdims=True)
    last = jnp.max(jnp.where(here, i, -1), axis=1, keepdims=True)
    place1 = jnp.sum(jnp.where(i == first, place, 0), axis=1, keepdims=True)
    place2 = jnp.sum(jnp.where(i == last, place, 0), axis=1, keepdims=True)
    place1 = spread(jnp.where(first < amount, place1, empty))
    pick1 = spread(jnp.where(first < amount, first, 0))
    twice = spread(jnp.where(last > first, 1, 0))
    place2, last = spread(place2), spread(last)
    lane = lax.broadcasted_iota(jnp.int32, wide, 2)
    r = lax.broadcasted_iota(jnp.int32, wide, 1)
    rank = jnp.zeros(wide, jnp.int32)
    for q in range(rows_n - 1):
        rank = rank + jnp.where(r > q, twice[:, q : q + 1, :], 0)
    few = jnp.where((rank == lane) & (lane < FEW), twice, 0)
    firsts = lane - 8 == r
    left = jnp.where(rank >= FEW, twice, 0)

    def down(value):
        return jnp.sum(value, axis=1, keepdims=True)

    row_lane = lax.broadcasted_iota(jnp.int32, (fronts, 1, 128), 2)
    over = jnp.sum(down(left), axis=0, keepdims=True)
    code = down(few * (r * empty + place2)) + down(jnp.where(firsts, place1, 0))
    code = jnp.where((row_lane < FEW) & (down(few) == 0), rows_n * empty, code)
    codes[...] = jnp.where(row_lane == FEW, over, code)
    picks[...] = down(few * last) + down(jnp.where(firsts, pick1, 0))
    idx3[...] = (left * last).reshape(dests, 128)
    place3[...] = jnp.where(left > 0, place2, empty).reshape(dests, 128)


def remote(src, dst, ssem, rsem, dev):
    return pltpu.make_async_remote_copy(src, dst, ssem, rsem, device_id=dev, device_id_type=MESH)


def level_kernel(fronts, rows_n, col_tiles, target, crow, ccol, owner, live, tiles_hbm, fown, wown_hbm, update,
                 inc, xin, places, over, base, panel, idx3, place3,
                 tiles, send, xsend, send2, in2, codes, picks, incode, pick_s, code_s,
                 fownv, fother, fcols, wown, wother, old, own_panel, half_panel, xcodes, ycodes,
                 ssem, rsem, xssem, xrsem, cssem, crsem, yssem, yrsem, ts, tr, cs, cr, ys, yr, xs, xr, ks, kr, ws, wr, wks, wkr, lsem):
    dests = fronts * rows_n
    empty = 4 * col_tiles
    front, row, col = lax.axis_index("front"), lax.axis_index("row"), lax.axis_index("col")
    me = front * rows_n + row
    x, k = row // 2, row % 2
    place_bits = empty.bit_length() - 1
    j = (x + 4 - 2 * col) % 4
    step_rows = fown.shape[0] // CHUNKS

    def at_j(place):
        return (front, ((place + 2 * col) % 4) * 2 + k, col)

    here = (front, row, col)
    mate = (front, x * 2 + 1 - k, col)
    across = (front, row, 1 - col)

    def part(i):
        return pl.ds(i * step_rows, step_rows)

    def load(n, src, dst):
        return pltpu.make_async_copy(src, dst, lsem.at[n])

    loads = [load(0, tiles_hbm, tiles), load(1, fown, fownv), load(2, wown_hbm, wown), load(3, update, old)]

    @pl.loop(0, CHUNKS)
    def _(i):
        remote(fown.at[part(i)], fother.at[part(i)], ys, yr.at[i], across).start()

    def give(which, half, i, src, dev):
        b = 2 * which + k
        remote(src, fcols.at[b, half, part(i)], xs, xr.at[which, half, i], dev).start()

    def to_mate(which, half, i, src):
        b = 2 * which + k
        remote(src, fcols.at[b, half, part(i)], ks, kr.at[which], mate).start()

    def own_out(half, i, src):
        @pl.when(j == 0)
        def _():
            give(0, half, i, src, at_j(3))
            give(0, half, i, src, at_j(1))
            to_mate(0, half, i, src)

        @pl.when(j == 1)
        def _():
            give(1, half, i, src, at_j(2))
            give(1, half, i, src, at_j(0))
            to_mate(1, half, i, src)

    @pl.loop(0, CHUNKS)
    def _(i):
        own_out(col, i, fown.at[part(i)])

    w_rows = wother.shape[0] // 2
    w_mine = pl.ds(pl.multiple_of(k * w_rows, TILE), w_rows)
    remote(wown_hbm.at[w_mine], wother.at[w_mine], ws, wr, across).start()
    for c in loads:
        c.start()

    make_tables(fronts, rows_n, col_tiles, target, crow, ccol, owner, codes, picks, idx3, place3)
    table = load(4, picks, pick_s)
    table.start()
    table.wait()
    loads[0].wait()

    for t in range(FEW):
        in2[front * FEW + t] = tiles[pick_s[front, 0, t]]
    incode[front] = codes[front]

    @pl.loop(1, fronts)
    def _(s):
        f = jnp.bitwise_xor(front, (s * 7) % fronts)
        for t in range(FEW):
            send2[f * FEW + t] = tiles[pick_s[f, 0, t]]
        dev = (f, row, col)
        remote(send2.at[pl.ds(f * FEW, FEW)], in2.at[pl.ds(front * FEW, FEW)], ts, tr, dev).start()
        remote(codes.at[f], incode.at[front], cs, cr, dev).start()

    send[me] = tiles[pick_s[front, 0, 8 + row]]
    own = load(5, send.at[me], inc.at[me])
    own.start()

    def arrived(which, half, i):
        b = 2 * which + k
        remote(fcols.at[b, half, part(i)], fcols.at[b, half, part(i)], xs, xr.at[which, half, i], mate).wait_recv()

    def pass_on(which, half, i, dev):
        b = 2 * which + k
        src = fcols.at[b, half, part(i)]
        if dev is not None:
            give(which, half, i, src, dev)
        to_mate(which, half, i, src)

    def straight(n):
        p = jnp.bitwise_xor(me, (n * 37) % dests)
        f, r = p // rows_n, p % rows_n
        send[p] = tiles[pick_s[f, 0, 8 + r]]
        remote(send.at[p], inc.at[me], ssem, rsem, (f, r, col)).start()

    per = EARLY // (2 * CHUNKS)

    @pl.loop(0, 2 * CHUNKS + 1)
    def _(s):
        @pl.when(s < 2 * CHUNKS)
        def _():
            @pl.loop(0, per)
            def _(inner):
                n = s * per + inner

                @pl.when(n > 0)
                def _():
                    straight(n)

            late = s // CHUNKS
            half = (col + late) % 2
            i = s % CHUNKS

            @pl.when(late == 1)
            def _():
                remote(fown.at[part(i)], fother.at[part(i)], ys, yr.at[i], across).wait_recv()
                own_out(half, i, fother.at[part(i)])

            @pl.when(s == CHUNKS)
            def _():
                whalf = remote(wother.at[w_mine], wother.at[w_mine], wks, wr, mate)
                whalf.wait_recv()
                remote(wother.at[w_mine], wother.at[w_mine], wks, wkr, mate).start()

            @pl.when(j == 0)
            def _():
                arrived(1, half, i)
                pass_on(1, half, i, None)

            @pl.when(j == 1)
            def _():
                arrived(0, half, i)
                pass_on(0, half, i, None)

            @pl.when(j == 2)
            def _():
                arrived(1, half, i)
                pass_on(1, half, i, at_j(3))

            @pl.when(j == 3)
            def _():
                arrived(0, half, i)
                pass_on(0, half, i, at_j(2))

        @pl.when(s > 0)
        def _():
            half = (col + (s - 1) // CHUNKS) % 2
            i = (s - 1) % CHUNKS

            @pl.when(j == 2)
            def _():
                arrived(0, half, i)
                pass_on(0, half, i, None)

            @pl.when(j == 3)
            def _():
                arrived(1, half, i)
                pass_on(1, half, i, None)

    some = pl.ds(0, (fronts - 1) * FEW)
    both = remote(send2.at[some], in2.at[some], ts, tr, mate)
    both.wait_send()
    both.wait_recv()
    most = pl.ds(0, fronts - 1)
    got = remote(codes.at[most], incode.at[most], cs, cr, mate)
    got.wait_send()
    got.wait_recv()
    table = load(4, incode, code_s)
    table.start()
    table.wait()

    def pack_one(r, g):
        t = 0
        for q in range(1, FEW):
            t = jnp.where(lax.shift_right_logical(code_s[g, 0, q], place_bits) == r, q, t)
        xsend[r * fronts + g] = in2[g * FEW + t]

    @pl.loop(0, rows_n)
    def _(s):
        r = jnp.bitwise_xor(row, s)

        @pl.when(s > 0)
        def _():
            remote(incode, xcodes.at[row], cssem, crsem, (front, r, col)).start()

        remote(incode, ycodes.at[row], yssem, yrsem, (front, r, 1 - col)).start()

    then = (dests - EARLY) // (rows_n - 1)

    @pl.loop(1, rows_n)
    def _(s):
        r = jnp.bitwise_xor(row, s)

        @pl.loop(0, fronts)
        def _(g):
            pack_one(r, g)

        src = xsend.at[pl.ds(r * fronts, fronts)]
        remote(src, xin.at[pl.ds(row * fronts, fronts)], xssem, xrsem, (front, r, col)).start()

        @pl.loop(0, then)
        def _(q):
            straight(EARLY + (s - 1) * then + q)

    @pl.loop(0, fronts)
    def _(g):
        pack_one(row, g)

    mine = pl.ds(row * fronts, fronts)
    ownx = load(4, xsend.at[mine], xin.at[mine])
    ownx.start()
    xcodes[row] = incode[...]

    for which in range(2):
        b = 2 * which + 1 - k
        remote(fcols.at[b], fcols.at[b], ks, kr.at[which], mate).wait_recv()
    w_other = pl.ds(pl.multiple_of((1 - k) * w_rows, TILE), w_rows)
    remote(wother.at[w_other], wother.at[w_other], wks, wkr, mate).wait_recv()
    for c in loads[1:]:
        c.wait()

    @pl.when(j < 2)
    def _():
        b = 2 * j + k
        fcols[b, col] = fownv[...]
        fcols[b, 1 - col] = fother[...]

    schur_base(live, fownv, fother, fcols, wown, wother, old, own_panel, half_panel)
    results = [load(1, old, base), load(2, half_panel, panel)]
    for c in results:
        c.start()


    some = pl.ds(0, rows_n - 1)
    both = remote(xcodes.at[some], xcodes.at[some], cssem, crsem, here)
    both.wait_send()
    both.wait_recv()
    both = remote(ycodes, ycodes, yssem, yrsem, here)
    both.wait_send()
    both.wait_recv()
    lane = lax.broadcasted_iota(jnp.int32, (fronts, 1, 128), 2)
    slot = lax.broadcasted_iota(jnp.int32, (fronts, 1, 128), 0)
    left = jnp.zeros((fronts, 1, 128), jnp.int32)
    for r in range(rows_n):
        code = xcodes[r]
        left = left + code + ycodes[r]
        one = jnp.sum(jnp.where(lane == 8 + row, code, 0), axis=2, keepdims=True)
        match = (lane < FEW) & (lax.shift_right_logical(code, place_bits) == row)
        two = jnp.min(jnp.where(match, code & (empty - 1), empty), axis=2, keepdims=True)
        places[r] = jnp.sum(jnp.where(lane == slot, one, 0) + jnp.where(lane == slot + fronts, two, 0), axis=0)
    over[0] = jnp.sum(jnp.where(lane == FEW, left, 0))

    remote(fown, fother, ys, yr.at[0], across).wait_send()
    remote(wother.at[w_mine], wother.at[w_mine], ws, wr, across).wait_send()
    remote(wother.at[w_mine], wother.at[w_mine], wks, wkr, mate).wait_send()
    pairs = fcols.at[pl.ds(0, 2)]
    remote(pairs, pairs, ks, kr.at[0], mate).wait_send()

    @pl.when(j < 2)
    def _():
        remote(pairs, pairs, xs, kr.at[0], mate).wait_send()

    @pl.when(j >= 2)
    def _():
        remote(fcols.at[0], fcols.at[0], xs, kr.at[0], mate).wait_send()

    own.wait()
    ownx.wait()
    for c in results:
        c.wait()
    some = pl.ds(0, dests - 1)
    both = remote(send.at[some], inc.at[some], ssem, rsem, here)
    both.wait_send()
    both.wait_recv()
    some = pl.ds(0, (rows_n - 1) * fronts)
    both = remote(xsend.at[some], xin.at[some], xssem, xrsem, here)
    both.wait_send()
    both.wait_recv()


def further_kernel(fronts, rows_n, idx, lab, tiles, inc, inlab, send, ssem, rsem, lssem, lrsem, lsem):
    dests = fronts * rows_n
    front, row, col = lax.axis_index("front"), lax.axis_index("row"), lax.axis_index("col")
    me = front * rows_n + row
    send[me] = tiles[idx[me]]
    own = pltpu.make_async_copy(send.at[me], inc.at[me], lsem.at[0])
    own.start()
    ownlab = pltpu.make_async_copy(lab.at[me], inlab.at[me], lsem.at[1])
    ownlab.start()

    @pl.loop(1, dests)
    def _(n):
        p = jnp.bitwise_xor(me, (n * 37) % dests)
        dev = (p // rows_n, p % rows_n, col)
        send[p] = tiles[idx[p]]
        remote(send.at[p], inc.at[me], ssem, rsem, dev).start()
        remote(lab.at[p], inlab.at[me], lssem, lrsem, dev).start()

    own.wait()
    ownlab.wait()
    some = pl.ds(0, dests - 1)
    both = remote(send.at[some], inc.at[some], ssem, rsem, (front, row, col))
    both.wait_send()
    both.wait_recv()
    labs = remote(lab.at[some], inlab.at[some], lssem, lrsem, (front, row, col))
    labs.wait_send()
    labs.wait_recv()


def add_tile(out, place, col_tiles, tile):
    @pl.when(place < 4 * col_tiles)
    def _():
        r = pl.multiple_of((place // col_tiles) * TILE, TILE)
        c = pl.multiple_of((place % col_tiles) * TILE, TILE)
        out[pl.ds(r, TILE), pl.ds(c, TILE)] += tile[...].astype(jnp.float32)


def more_kernel(group, col_tiles, lab, base, tiles, out):
    step = pl.program_id(0)

    @pl.when(step == 0)
    def _():
        out[...] = base[...]

    @pl.loop(0, group)
    def _(i):
        add_tile(out, lab[step * group + i, 0, 0], col_tiles, tiles.at[i])


def finish_kernel(fronts, rows_n, col_tiles, places, live, base, first, second, panel, out, panel_out,
                  fbuf, sbuf, total, obuf, fsem, ssem, osem, psem, bsem):
    row, col = lax.axis_index("row"), lax.axis_index("col")
    bound = live[0] * TILE
    height, width = total.shape
    copy = pltpu.make_async_copy

    def tiles_of(r):
        part = pl.ds(r * fronts, fronts)
        return copy(first.at[part], fbuf.at[part], fsem.at[r]), copy(second.at[part], sbuf.at[part], ssem.at[r])

    fill = copy(base, total, bsem)
    fill.start()
    for r in range(rows_n):
        for c in tiles_of(r):
            c.start()
    copy(panel, panel_out, psem).start()
    fill.wait()

    @pl.loop(0, rows_n)
    def _(s):
        for c in tiles_of(s):
            c.wait()
        for i in range(fronts):
            front = s * (fronts // rows_n) + i // rows_n
            add_tile(total, places[i % rows_n, 0, front], col_tiles, fbuf.at[s * fronts + i])
            add_tile(total, places[s, 0, fronts + i], col_tiles, sbuf.at[s * fronts + i])

    def rows_out(i):
        rows = pl.ds(pl.multiple_of(i * TILE, TILE), TILE)
        return copy(obuf.at[rows], out.at[rows], osem.at[i])

    @pl.loop(0, height // TILE)
    def _(i):
        rows = pl.ds(pl.multiple_of(i * TILE, TILE), TILE)
        row_ids = row * height + i * TILE + lax.broadcasted_iota(jnp.int32, (TILE, 1), 0)
        col_ids = col * width + lax.broadcasted_iota(jnp.int32, (1, width), 1)
        inside = (row_ids < bound) & (col_ids < bound)
        obuf[rows] = jnp.where(inside, total[rows], 0.0).astype(obuf.dtype)
        rows_out(i).start()

    @pl.loop(0, height // TILE)
    def _(i):
        rows_out(i).wait()

    copy(panel, panel_out, psem).wait()


def per_device(
    update_block,
    front_panel,
    inverse_factor,
    child_tiles,
    child_target,
    child_row,
    child_col,
    front_owner,
    live_tiles,
):
    rows_dev = update_block.shape[1]
    cols_dev = update_block.shape[2]
    fronts = lax.axis_size("front")
    rows_n = lax.axis_size("row")
    dests = fronts * rows_n
    col_tiles = cols_dev // TILE
    half = front_panel.shape[2]

    anyspace = pl.BlockSpec(memory_space=pl.ANY)
    hbm = pl.BlockSpec(memory_space=pltpu.HBM)
    smem = pl.BlockSpec(memory_space=pltpu.SMEM)
    vmem = pl.BlockSpec(memory_space=pltpu.VMEM)
    shape = jax.ShapeDtypeStruct
    tile_shape = (TILE, TILE)
    ints = lambda *s: shape(s, jnp.int32)
    params = pltpu.CompilerParams(has_side_effects=True, vmem_limit_bytes=40 << 20)

    block = (rows_dev, cols_dev)
    group = dests // rows_n
    inc_shape = shape((dests,) + tile_shape, jnp.bfloat16)
    rows_buf = lambda *n: pltpu.VMEM(n + (rows_dev, half), jnp.float32)
    tiles_buf = lambda n: pltpu.VMEM((n,) + tile_shape, jnp.bfloat16)
    table = lambda space: space((fronts, 1, 128), jnp.int32)
    amount = child_tiles.shape[0]
    first, second, places, over, base, panel_half, idx3, place3 = pl.pallas_call(
        functools.partial(level_kernel, fronts, rows_n, col_tiles),
        out_shape=(inc_shape, inc_shape, ints(rows_n, 1, 128), ints(1), shape(block, jnp.float32),
                   shape((rows_dev, half), jnp.float32), ints(dests, 128), ints(dests, 128)),
        in_specs=[vmem, vmem, vmem, smem, smem, anyspace, anyspace, anyspace, anyspace],
        out_specs=(hbm, hbm, vmem, smem, hbm, hbm, vmem, vmem),
        scratch_shapes=[
            tiles_buf(amount), tiles_buf(dests), tiles_buf(dests), tiles_buf(fronts * FEW), tiles_buf(fronts * FEW),
            table(pltpu.VMEM), table(pltpu.VMEM), table(pltpu.VMEM), table(pltpu.SMEM), table(pltpu.SMEM),
            rows_buf(), rows_buf(), rows_buf(4, 2),
            pltpu.VMEM((2 * half, half), jnp.float32), pltpu.VMEM((2 * half, half), jnp.float32),
            pltpu.VMEM(block, jnp.float32), pltpu.VMEM((rows_dev, 2 * half), jnp.float32), rows_buf(),
            pltpu.VMEM((rows_n, fronts, 1, 128), jnp.int32), pltpu.VMEM((rows_n, fronts, 1, 128), jnp.int32),
        ] + [DMA] * 13 + [DMA((CHUNKS,)), DMA, DMA((2, 2, CHUNKS)), DMA, DMA((2,))] + [DMA] * 4 + [DMA((6,))],
        compiler_params=pltpu.CompilerParams(has_side_effects=True, vmem_limit_bytes=58 << 20),
        cost_estimate=pl.CostEstimate(flops=0, bytes_accessed=300_000_000, transcendentals=0),
        name="level",
    )(child_target.reshape(1, amount), child_row.reshape(1, amount), child_col.reshape(1, amount), front_owner, live_tiles,
      child_tiles, front_panel[0], inverse_factor[0], update_block[0])

    whole = pl.BlockSpec(block, lambda i: (0, 0), pipeline_mode=pl.Buffered(1))
    tiles_spec = pl.BlockSpec((group,) + tile_shape, lambda i: (i, 0, 0))

    def further(value):
        labels = jnp.broadcast_to(place3[:, :1, None], (dests, 1, 128))
        tiles3, labels3 = pl.pallas_call(
            functools.partial(further_kernel, fronts, rows_n),
            out_shape=(inc_shape, ints(dests, 1, 128)),
            in_specs=[smem, anyspace, vmem],
            out_specs=(anyspace,) * 2,
            scratch_shapes=[tiles_buf(dests)] + [DMA] * 4 + [DMA((2,))],
            compiler_params=params,
            name="further",
        )(idx3[:, 0], labels, child_tiles)
        return pl.pallas_call(
            functools.partial(more_kernel, group, col_tiles),
            out_shape=shape(block, jnp.float32),
            grid=(rows_n,),
            in_specs=[smem, whole, tiles_spec],
            out_specs=pl.BlockSpec(block, lambda i: (0, 0)),
            compiler_params=pltpu.CompilerParams(vmem_limit_bytes=40 << 20),
            name="more",
        )(labels3, value, tiles3)

    base = lax.cond(over[0] > 0, further, lambda value: value, base)

    schur_out, panel_out = pl.pallas_call(
        functools.partial(finish_kernel, fronts, rows_n, col_tiles),
        out_shape=(shape(block, jnp.bfloat16), shape((rows_dev, half), jnp.float32)),
        in_specs=[smem, smem, hbm, hbm, hbm, vmem],
        out_specs=(hbm, hbm),
        scratch_shapes=[
            tiles_buf(dests), tiles_buf(dests), pltpu.VMEM(block, jnp.float32), pltpu.VMEM(block, jnp.bfloat16),
            DMA((rows_n,)), DMA((rows_n,)), DMA((rows_dev // TILE,)), DMA, DMA,
        ],
        compiler_params=pltpu.CompilerParams(vmem_limit_bytes=58 << 20),
        name="finish",
    )(places, live_tiles, base, first, second, panel_half)
    return (schur_out[None], panel_out[None])


def solution(mesh):
    return jax.shard_map(
        per_device,
        mesh=mesh,
        in_specs=(
            P("front", "row", "col"),
            P("front", "row", "col"),
            P("front", None, "col"),
            P(("front", "row", "col"), None, None),
            P(("front", "row", "col"), None),
            P(("front", "row", "col")),
            P(("front", "row", "col")),
            P(),
            P("front"),
        ),
        out_specs=(P("front", "row", "col"), P("front", "row", "col")),
        check_vma=False,
    )
```

```python
import functools

import jax
import jax.numpy as jnp
from jax import lax
from jax.experimental import pallas as pl
from jax.experimental.pallas import tpu as pltpu
from jax.sharding import PartitionSpec as P

TILE = 128
FEW = 3
EARLY = 72
CHUNKS = 2
MESH = pl.DeviceIdType.MESH
DMA = pltpu.SemaphoreType.DMA


def schur_base(live, fown, fother, fcols, wown, wother, update, own_panel, panel):
    row, col = lax.axis_index("row"), lax.axis_index("col")
    height, width = update.shape
    half = fown.shape[1]
    step = height // 2
    bound = live[0] * TILE
    mine = pl.ds(pl.multiple_of(col * half, TILE), half)

    def times(a, b):
        return lax.dot_general(
            a, b, (((1,), (1,)), ((), ())), precision=lax.Precision.HIGHEST, preferred_element_type=jnp.float32
        )

    def panel_rows(a, b, start):
        value = times(a, wown[...]) + times(b, wother[...])
        ids = start + lax.broadcasted_iota(jnp.int32, value.shape, 0)
        return jnp.where(ids < bound, value, 0.0)

    @pl.loop(0, 2)
    def _(i):
        rows = pl.ds(pl.multiple_of(i * step, step), step)
        own_panel[rows] = panel_rows(fown[rows], fother[rows], row * height + i * step)

    panel[...] = own_panel[:, mine]

    @pl.loop(0, width // step)
    def _(c):
        rows = pl.ds(pl.multiple_of((c % 2) * step, step), step)
        value = panel_rows(fcols[c // 2, col, rows], fcols[c // 2, 1 - col, rows], col * width + c * step)
        lanes = pl.ds(pl.multiple_of(c * step, step), step)
        update[:, lanes] = update[:, lanes] - times(own_panel[...], value)


def make_tables(fronts, rows_n, col_tiles, target, crow, ccol, owner, codes, picks, idx3, place3):
    dests = fronts * rows_n
    empty = 4 * col_tiles
    bits = rows_n.bit_length() - 1
    amount = target.shape[1]
    t = target[...]
    holder = jnp.zeros_like(t)
    for f in range(fronts):
        holder = jnp.where(lax.shift_right_arithmetic(t, bits) == f, owner[f], holder)
    address = holder * rows_n + (t & (rows_n - 1))
    place = crow[...] * col_tiles + ccol[...]
    grid = (dests, amount)
    i = lax.broadcasted_iota(jnp.int32, grid, 1)
    here = lax.broadcasted_iota(jnp.int32, grid, 0) == address
    wide = (fronts, rows_n, 128)

    def spread(column):
        return jnp.broadcast_to(column, (dests, 128)).reshape(wide)

    first = jnp.min(jnp.where(here, i, amount), axis=1, keepdims=True)
    last = jnp.max(jnp.where(here, i, -1), axis=1, keepdims=True)
    place1 = jnp.sum(jnp.where(i == first, place, 0), axis=1, keepdims=True)
    place2 = jnp.sum(jnp.where(i == last, place, 0), axis=1, keepdims=True)
    place1 = spread(jnp.where(first < amount, place1, empty))
    pick1 = spread(jnp.where(first < amount, first, 0))
    twice = spread(jnp.where(last > first, 1, 0))
    place2, last = spread(place2), spread(last)
    lane = lax.broadcasted_iota(jnp.int32, wide, 2)
    r = lax.broadcasted_iota(jnp.int32, wide, 1)
    rank = jnp.zeros(wide, jnp.int32)
    for q in range(rows_n - 1):
        rank = rank + jnp.where(r > q, twice[:, q : q + 1, :], 0)
    few = jnp.where((rank == lane) & (lane < FEW), twice, 0)
    firsts = lane - 8 == r
    left = jnp.where(rank >= FEW, twice, 0)

    def down(value):
        return jnp.sum(value, axis=1, keepdims=True)

    row_lane = lax.broadcasted_iota(jnp.int32, (fronts, 1, 128), 2)
    over = jnp.sum(down(left), axis=0, keepdims=True)
    code = down(few * (r * empty + place2)) + down(jnp.where(firsts, place1, 0))
    code = jnp.where((row_lane < FEW) & (down(few) == 0), rows_n * empty, code)
    codes[...] = jnp.where(row_lane == FEW, over, code)
    picks[...] = down(few * last) + down(jnp.where(firsts, pick1, 0))
    idx3[...] = (left * last).reshape(dests, 128)
    place3[...] = jnp.where(left > 0, place2, empty).reshape(dests, 128)


def remote(src, dst, ssem, rsem, dev):
    return pltpu.make_async_remote_copy(src, dst, ssem, rsem, device_id=dev, device_id_type=MESH)


def level_kernel(fronts, rows_n, col_tiles, target, crow, ccol, owner, live, tiles_hbm, fown, wown_hbm, update,
                 inc, xin, places, over, base, panel, idx3, place3,
                 tiles, send, xsend, send2, in2, codes, picks, incode, pick_s, code_s,
                 fownv, fother, fcols, wown, wother, old, own_panel, half_panel, xcodes, ycodes,
                 ssem, rsem, xssem, xrsem, cssem, crsem, yssem, yrsem, ts, tr, cs, cr, ys, yr, xs, xr, ks, kr, ws, wr, wks, wkr, lsem):
    dests = fronts * rows_n
    empty = 4 * col_tiles
    front, row, col = lax.axis_index("front"), lax.axis_index("row"), lax.axis_index("col")
    me = front * rows_n + row
    x, k = row // 2, row % 2
    place_bits = empty.bit_length() - 1
    j = (x + 4 - 2 * col) % 4
    step_rows = fown.shape[0] // CHUNKS

    def at_j(place):
        return (front, ((place + 2 * col) % 4) * 2 + k, col)

    here = (front, row, col)
    mate = (front, x * 2 + 1 - k, col)
    across = (front, row, 1 - col)

    def part(i):
        return pl.ds(i * step_rows, step_rows)

    def load(n, src, dst):
        return pltpu.make_async_copy(src, dst, lsem.at[n])

    loads = [load(0, tiles_hbm, tiles), load(1, fown, fownv), load(2, wown_hbm, wown), load(3, update, old)]

    @pl.loop(0, CHUNKS)
    def _(i):
        remote(fown.at[part(i)], fother.at[part(i)], ys, yr.at[i], across).start()

    def give(which, half, i, src, dev):
        b = 2 * which + k
        remote(src, fcols.at[b, half, part(i)], xs, xr.at[which, half, i], dev).start()

    def to_mate(which, half, i, src):
        b = 2 * which + k
        remote(src, fcols.at[b, half, part(i)], ks, kr.at[which], mate).start()

    def own_out(half, i, src):
        @pl.when(j == 0)
        def _():
            give(0, half, i, src, at_j(3))
            give(0, half, i, src, at_j(1))
            to_mate(0, half, i, src)

        @pl.when(j == 1)
        def _():
            give(1, half, i, src, at_j(2))
            give(1, half, i, src, at_j(0))
            to_mate(1, half, i, src)

    @pl.loop(0, CHUNKS)
    def _(i):
        own_out(col, i, fown.at[part(i)])

    w_rows = wother.shape[0] // 2
    w_mine = pl.ds(pl.multiple_of(k * w_rows, TILE), w_rows)
    remote(wown_hbm.at[w_mine], wother.at[w_mine], ws, wr, across).start()
    for c in loads:
        c.start()

    make_tables(fronts, rows_n, col_tiles, target, crow, ccol, owner, codes, picks, idx3, place3)
    table = load(4, picks, pick_s)
    table.start()
    table.wait()
    loads[0].wait()

    for t in range(FEW):
        in2[front * FEW + t] = tiles[pick_s[front, 0, t]]
    incode[front] = codes[front]

    @pl.loop(1, fronts)
    def _(s):
        f = jnp.bitwise_xor(front, (s * 7) % fronts)
        for t in range(FEW):
            send2[f * FEW + t] = tiles[pick_s[f, 0, t]]
        dev = (f, row, col)
        remote(send2.at[pl.ds(f * FEW, FEW)], in2.at[pl.ds(front * FEW, FEW)], ts, tr, dev).start()
        remote(codes.at[f], incode.at[front], cs, cr, dev).start()

    send[me] = tiles[pick_s[front, 0, 8 + row]]
    own = load(5, send.at[me], inc.at[me])
    own.start()

    def arrived(which, half, i):
        b = 2 * which + k
        remote(fcols.at[b, half, part(i)], fcols.at[b, half, part(i)], xs, xr.at[which, half, i], mate).wait_recv()

    def pass_on(which, half, i, dev):
        b = 2 * which + k
        src = fcols.at[b, half, part(i)]
        if dev is not None:
            give(which, half, i, src, dev)
        to_mate(which, half, i, src)

    def straight(n):
        p = jnp.bitwise_xor(me, (n * 37) % dests)
        f, r = p // rows_n, p % rows_n
        send[p] = tiles[pick_s[f, 0, 8 + r]]
        remote(send.at[p], inc.at[me], ssem, rsem, (f, r, col)).start()

    per = EARLY // (2 * CHUNKS)

    @pl.loop(0, 2 * CHUNKS + 1)
    def _(s):
        @pl.when(s < 2 * CHUNKS)
        def _():
            @pl.loop(0, per)
            def _(inner):
                n = s * per + inner

                @pl.when(n > 0)
                def _():
                    straight(n)

            late = s // CHUNKS
            half = (col + late) % 2
            i = s % CHUNKS

            @pl.when(late == 1)
            def _():
                remote(fown.at[part(i)], fother.at[part(i)], ys, yr.at[i], across).wait_recv()
                own_out(half, i, fother.at[part(i)])

            @pl.when(s == CHUNKS)
            def _():
                whalf = remote(wother.at[w_mine], wother.at[w_mine], wks, wr, mate)
                whalf.wait_recv()
                remote(wother.at[w_mine], wother.at[w_mine], wks, wkr, mate).start()

            @pl.when(j == 0)
            def _():
                arrived(1, half, i)
                pass_on(1, half, i, None)

            @pl.when(j == 1)
            def _():
                arrived(0, half, i)
                pass_on(0, half, i, None)

            @pl.when(j == 2)
            def _():
                arrived(1, half, i)
                pass_on(1, half, i, at_j(3))

            @pl.when(j == 3)
            def _():
                arrived(0, half, i)
                pass_on(0, half, i, at_j(2))

        @pl.when(s > 0)
        def _():
            half = (col + (s - 1) // CHUNKS) % 2
            i = (s - 1) % CHUNKS

            @pl.when(j == 2)
            def _():
                arrived(0, half, i)
                pass_on(0, half, i, None)

            @pl.when(j == 3)
            def _():
                arrived(1, half, i)
                pass_on(1, half, i, None)

    some = pl.ds(0, (fronts - 1) * FEW)
    both = remote(send2.at[some], in2.at[some], ts, tr, mate)
    both.wait_send()
    both.wait_recv()
    most = pl.ds(0, fronts - 1)
    got = remote(codes.at[most], incode.at[most], cs, cr, mate)
    got.wait_send()
    got.wait_recv()
    table = load(4, incode, code_s)
    table.start()
    table.wait()

    def pack_one(r, g):
        t = 0
        for q in range(1, FEW):
            t = jnp.where(lax.shift_right_logical(code_s[g, 0, q], place_bits) == r, q, t)
        xsend[r * fronts + g] = in2[g * FEW + t]

    @pl.loop(0, rows_n)
    def _(s):
        r = jnp.bitwise_xor(row, s)

        @pl.when(s > 0)
        def _():
            remote(incode, xcodes.at[row], cssem, crsem, (front, r, col)).start()

        remote(incode, ycodes.at[row], yssem, yrsem, (front, r, 1 - col)).start()

    then = (dests - EARLY) // (rows_n - 1)

    @pl.loop(1, rows_n)
    def _(s):
        r = jnp.bitwise_xor(row, s)

        @pl.loop(0, fronts)
        def _(g):
            pack_one(r, g)

        src = xsend.at[pl.ds(r * fronts, fronts)]
        remote(src, xin.at[pl.ds(row * fronts, fronts)], xssem, xrsem, (front, r, col)).start()

        @pl.loop(0, then)
        def _(q):
            straight(EARLY + (s - 1) * then + q)

    @pl.loop(0, fronts)
    def _(g):
        pack_one(row, g)

    mine = pl.ds(row * fronts, fronts)
    ownx = load(4, xsend.at[mine], xin.at[mine])
    ownx.start()
    xcodes[row] = incode[...]

    for which in range(2):
        b = 2 * which + 1 - k
        remote(fcols.at[b], fcols.at[b], ks, kr.at[which], mate).wait_recv()
    w_other = pl.ds(pl.multiple_of((1 - k) * w_rows, TILE), w_rows)
    remote(wother.at[w_other], wother.at[w_other], wks, wkr, mate).wait_recv()
    for c in loads[1:]:
        c.wait()

    @pl.when(j < 2)
    def _():
        b = 2 * j + k
        fcols[b, col] = fownv[...]
        fcols[b, 1 - col] = fother[...]

    schur_base(live, fownv, fother, fcols, wown, wother, old, own_panel, half_panel)
    results = [load(1, old, base), load(2, half_panel, panel)]
    for c in results:
        c.start()


    some = pl.ds(0, rows_n - 1)
    both = remote(xcodes.at[some], xcodes.at[some], cssem, crsem, here)
    both.wait_send()
    both.wait_recv()
    both = remote(ycodes, ycodes, yssem, yrsem, here)
    both.wait_send()
    both.wait_recv()
    lane = lax.broadcasted_iota(jnp.int32, (fronts, 1, 128), 2)
    slot = lax.broadcasted_iota(jnp.int32, (fronts, 1, 128), 0)
    left = jnp.zeros((fronts, 1, 128), jnp.int32)
    for r in range(rows_n):
        code = xcodes[r]
        left = left + code + ycodes[r]
        one = jnp.sum(jnp.where(lane == 8 + row, code, 0), axis=2, keepdims=True)
        match = (lane < FEW) & (lax.shift_right_logical(code, place_bits) == row)
        two = jnp.min(jnp.where(match, code & (empty - 1), empty), axis=2, keepdims=True)
        places[r] = jnp.sum(jnp.where(lane == slot, one, 0) + jnp.where(lane == slot + fronts, two, 0), axis=0)
    over[0] = jnp.sum(jnp.where(lane == FEW, left, 0))

    remote(fown, fother, ys, yr.at[0], across).wait_send()
    remote(wother.at[w_mine], wother.at[w_mine], ws, wr, across).wait_send()
    remote(wother.at[w_mine], wother.at[w_mine], wks, wkr, mate).wait_send()
    pairs = fcols.at[pl.ds(0, 2)]
    remote(pairs, pairs, ks, kr.at[0], mate).wait_send()

    @pl.when(j < 2)
    def _():
        remote(pairs, pairs, xs, kr.at[0], mate).wait_send()

    @pl.when(j >= 2)
    def _():
        remote(fcols.at[0], fcols.at[0], xs, kr.at[0], mate).wait_send()

    own.wait()
    ownx.wait()
    for c in results:
        c.wait()
    some = pl.ds(0, dests - 1)
    both = remote(send.at[some], inc.at[some], ssem, rsem, here)
    both.wait_send()
    both.wait_recv()
    some = pl.ds(0, (rows_n - 1) * fronts)
    both = remote(xsend.at[some], xin.at[some], xssem, xrsem, here)
    both.wait_send()
    both.wait_recv()


def further_kernel(fronts, rows_n, idx, lab, tiles, inc, inlab, send, ssem, rsem, lssem, lrsem, lsem):
    dests = fronts * rows_n
    front, row, col = lax.axis_index("front"), lax.axis_index("row"), lax.axis_index("col")
    me = front * rows_n + row
    send[me] = tiles[idx[me]]
    own = pltpu.make_async_copy(send.at[me], inc.at[me], lsem.at[0])
    own.start()
    ownlab = pltpu.make_async_copy(lab.at[me], inlab.at[me], lsem.at[1])
    ownlab.start()

    @pl.loop(1, dests)
    def _(n):
        p = jnp.bitwise_xor(me, (n * 37) % dests)
        dev = (p // rows_n, p % rows_n, col)
        send[p] = tiles[idx[p]]
        remote(send.at[p], inc.at[me], ssem, rsem, dev).start()
        remote(lab.at[p], inlab.at[me], lssem, lrsem, dev).start()

    own.wait()
    ownlab.wait()
    some = pl.ds(0, dests - 1)
    both = remote(send.at[some], inc.at[some], ssem, rsem, (front, row, col))
    both.wait_send()
    both.wait_recv()
    labs = remote(lab.at[some], inlab.at[some], lssem, lrsem, (front, row, col))
    labs.wait_send()
    labs.wait_recv()


def add_tile(out, place, col_tiles, tile):
    @pl.when(place < 4 * col_tiles)
    def _():
        r = pl.multiple_of((place // col_tiles) * TILE, TILE)
        c = pl.multiple_of((place % col_tiles) * TILE, TILE)
        out[pl.ds(r, TILE), pl.ds(c, TILE)] += tile[...].astype(jnp.float32)


def more_kernel(group, col_tiles, lab, base, tiles, out):
    step = pl.program_id(0)

    @pl.when(step == 0)
    def _():
        out[...] = base[...]

    @pl.loop(0, group)
    def _(i):
        add_tile(out, lab[step * group + i, 0, 0], col_tiles, tiles.at[i])


def finish_kernel(fronts, rows_n, col_tiles, places, live, base, first, second, panel, out, panel_out,
                  fbuf, sbuf, total, old, obuf, fsem, ssem, osem, psem, bsem):
    row, col = lax.axis_index("row"), lax.axis_index("col")
    bound = live[0] * TILE
    height, width = total.shape
    copy = pltpu.make_async_copy

    def tiles_of(r):
        part = pl.ds(r * fronts, fronts)
        return copy(first.at[part], fbuf.at[part], fsem.at[r]), copy(second.at[part], sbuf.at[part], ssem.at[r])

    for r in range(rows_n):
        for c in tiles_of(r):
            c.start()
    fill = copy(base, old, bsem)
    fill.start()
    copy(panel, panel_out, psem).start()
    total[...] = jnp.zeros_like(total)

    @pl.loop(0, rows_n)
    def _(s):
        for c in tiles_of(s):
            c.wait()
        for i in range(fronts):
            front = s * (fronts // rows_n) + i // rows_n
            add_tile(total, places[i % rows_n, 0, front], col_tiles, fbuf.at[s * fronts + i])
            add_tile(total, places[s, 0, fronts + i], col_tiles, sbuf.at[s * fronts + i])

    fill.wait()

    def rows_out(i):
        rows = pl.ds(pl.multiple_of(i * TILE, TILE), TILE)
        return copy(obuf.at[rows], out.at[rows], osem.at[i])

    @pl.loop(0, height // TILE)
    def _(i):
        rows = pl.ds(pl.multiple_of(i * TILE, TILE), TILE)
        row_ids = row * height + i * TILE + lax.broadcasted_iota(jnp.int32, (TILE, 1), 0)
        col_ids = col * width + lax.broadcasted_iota(jnp.int32, (1, width), 1)
        inside = (row_ids < bound) & (col_ids < bound)
        obuf[rows] = jnp.where(inside, old[rows] + total[rows], 0.0).astype(obuf.dtype)
        rows_out(i).start()

    @pl.loop(0, height // TILE)
    def _(i):
        rows_out(i).wait()

    copy(panel, panel_out, psem).wait()


def per_device(
    update_block,
    front_panel,
    inverse_factor,
    child_tiles,
    child_target,
    child_row,
    child_col,
    front_owner,
    live_tiles,
):
    rows_dev = update_block.shape[1]
    cols_dev = update_block.shape[2]
    fronts = lax.axis_size("front")
    rows_n = lax.axis_size("row")
    dests = fronts * rows_n
    col_tiles = cols_dev // TILE
    half = front_panel.shape[2]

    anyspace = pl.BlockSpec(memory_space=pl.ANY)
    hbm = pl.BlockSpec(memory_space=pltpu.HBM)
    smem = pl.BlockSpec(memory_space=pltpu.SMEM)
    vmem = pl.BlockSpec(memory_space=pltpu.VMEM)
    shape = jax.ShapeDtypeStruct
    tile_shape = (TILE, TILE)
    ints = lambda *s: shape(s, jnp.int32)
    params = pltpu.CompilerParams(has_side_effects=True, vmem_limit_bytes=40 << 20)

    block = (rows_dev, cols_dev)
    group = dests // rows_n
    inc_shape = shape((dests,) + tile_shape, jnp.bfloat16)
    rows_buf = lambda *n: pltpu.VMEM(n + (rows_dev, half), jnp.float32)
    tiles_buf = lambda n: pltpu.VMEM((n,) + tile_shape, jnp.bfloat16)
    table = lambda space: space((fronts, 1, 128), jnp.int32)
    amount = child_tiles.shape[0]
    first, second, places, over, base, panel_half, idx3, place3 = pl.pallas_call(
        functools.partial(level_kernel, fronts, rows_n, col_tiles),
        out_shape=(inc_shape, inc_shape, ints(rows_n, 1, 128), ints(1), shape(block, jnp.float32),
                   shape((rows_dev, half), jnp.float32), ints(dests, 128), ints(dests, 128)),
        in_specs=[vmem, vmem, vmem, smem, smem, anyspace, anyspace, anyspace, anyspace],
        out_specs=(hbm, hbm, vmem, smem, hbm, hbm, vmem, vmem),
        scratch_shapes=[
            tiles_buf(amount), tiles_buf(dests), tiles_buf(dests), tiles_buf(fronts * FEW), tiles_buf(fronts * FEW),
            table(pltpu.VMEM), table(pltpu.VMEM), table(pltpu.VMEM), table(pltpu.SMEM), table(pltpu.SMEM),
            rows_buf(), rows_buf(), rows_buf(4, 2),
            pltpu.VMEM((2 * half, half), jnp.float32), pltpu.VMEM((2 * half, half), jnp.float32),
            pltpu.VMEM(block, jnp.float32), pltpu.VMEM((rows_dev, 2 * half), jnp.float32), rows_buf(),
            pltpu.VMEM((rows_n, fronts, 1, 128), jnp.int32), pltpu.VMEM((rows_n, fronts, 1, 128), jnp.int32),
        ] + [DMA] * 13 + [DMA((CHUNKS,)), DMA, DMA((2, 2, CHUNKS)), DMA, DMA((2,))] + [DMA] * 4 + [DMA((6,))],
        compiler_params=pltpu.CompilerParams(has_side_effects=True, vmem_limit_bytes=58 << 20),
        cost_estimate=pl.CostEstimate(flops=0, bytes_accessed=300_000_000, transcendentals=0),
        name="level",
    )(child_target.reshape(1, amount), child_row.reshape(1, amount), child_col.reshape(1, amount), front_owner, live_tiles,
      child_tiles, front_panel[0], inverse_factor[0], update_block[0])

    whole = pl.BlockSpec(block, lambda i: (0, 0), pipeline_mode=pl.Buffered(1))
    tiles_spec = pl.BlockSpec((group,) + tile_shape, lambda i: (i, 0, 0))

    def further(value):
        labels = jnp.broadcast_to(place3[:, :1, None], (dests, 1, 128))
        tiles3, labels3 = pl.pallas_call(
            functools.partial(further_kernel, fronts, rows_n),
            out_shape=(inc_shape, ints(dests, 1, 128)),
            in_specs=[smem, anyspace, vmem],
            out_specs=(anyspace,) * 2,
            scratch_shapes=[tiles_buf(dests)] + [DMA] * 4 + [DMA((2,))],
            compiler_params=params,
            name="further",
        )(idx3[:, 0], labels, child_tiles)
        return pl.pallas_call(
            functools.partial(more_kernel, group, col_tiles),
            out_shape=shape(block, jnp.float32),
            grid=(rows_n,),
            in_specs=[smem, whole, tiles_spec],
            out_specs=pl.BlockSpec(block, lambda i: (0, 0)),
            compiler_params=pltpu.CompilerParams(vmem_limit_bytes=40 << 20),
            name="more",
        )(labels3, value, tiles3)

    base = lax.cond(over[0] > 0, further, lambda value: value, base)

    schur_out, panel_out = pl.pallas_call(
        functools.partial(finish_kernel, fronts, rows_n, col_tiles),
        out_shape=(shape(block, jnp.bfloat16), shape((rows_dev, half), jnp.float32)),
        in_specs=[smem, smem, hbm, hbm, hbm, vmem],
        out_specs=(hbm, hbm),
        scratch_shapes=[
            tiles_buf(dests), tiles_buf(dests), pltpu.VMEM(block, jnp.float32), pltpu.VMEM(block, jnp.float32),
            pltpu.VMEM(block, jnp.bfloat16),
            DMA((rows_n,)), DMA((rows_n,)), DMA((rows_dev // TILE,)), DMA, DMA,
        ],
        compiler_params=pltpu.CompilerParams(vmem_limit_bytes=58 << 20),
        name="finish",
    )(places, live_tiles, base, first, second, panel_half)
    return (schur_out[None], panel_out[None])


def solution(mesh):
    return jax.shard_map(
        per_device,
        mesh=mesh,
        in_specs=(
            P("front", "row", "col"),
            P("front", "row", "col"),
            P("front", None, "col"),
            P(("front", "row", "col"), None, None),
            P(("front", "row", "col"), None),
            P(("front", "row", "col")),
            P(("front", "row", "col")),
            P(),
            P("front"),
        ),
        out_specs=(P("front", "row", "col"), P("front", "row", "col")),
        check_vma=False,
    )
```

```python
import functools

import jax
import jax.numpy as jnp
from jax import lax
from jax.experimental import pallas as pl
from jax.experimental.pallas import tpu as pltpu
from jax.sharding import PartitionSpec as P

TILE = 128
FEW = 3
EARLY = 100
CHUNKS = 1
MESH = pl.DeviceIdType.MESH
DMA = pltpu.SemaphoreType.DMA


def schur_base(live, fown, fother, fcols, wown, wother, update, own_panel, panel):
    row, col = lax.axis_index("row"), lax.axis_index("col")
    height, width = update.shape
    half = fown.shape[1]
    step = height // 2
    bound = live[0] * TILE
    mine = pl.ds(pl.multiple_of(col * half, TILE), half)

    def times(a, b):
        return lax.dot_general(
            a, b, (((1,), (1,)), ((), ())), precision=lax.Precision.HIGHEST, preferred_element_type=jnp.float32
        )

    def panel_rows(a, b, start):
        value = times(a, wown[...]) + times(b, wother[...])
        ids = start + lax.broadcasted_iota(jnp.int32, value.shape, 0)
        return jnp.where(ids < bound, value, 0.0)

    @pl.loop(0, 2)
    def _(i):
        rows = pl.ds(pl.multiple_of(i * step, step), step)
        own_panel[rows] = panel_rows(fown[rows], fother[rows], row * height + i * step)

    panel[...] = own_panel[:, mine]

    @pl.loop(0, width // step)
    def _(c):
        rows = pl.ds(pl.multiple_of((c % 2) * step, step), step)
        value = panel_rows(fcols[c // 2, col, rows], fcols[c // 2, 1 - col, rows], col * width + c * step)
        lanes = pl.ds(pl.multiple_of(c * step, step), step)
        update[:, lanes] = update[:, lanes] - times(own_panel[...], value)


def make_tables(fronts, rows_n, col_tiles, target, crow, ccol, owner, codes, picks, idx3, place3):
    dests = fronts * rows_n
    empty = 4 * col_tiles
    bits = rows_n.bit_length() - 1
    amount = target.shape[1]
    t = target[...]
    holder = jnp.zeros_like(t)
    for f in range(fronts):
        holder = jnp.where(lax.shift_right_arithmetic(t, bits) == f, owner[f], holder)
    address = holder * rows_n + (t & (rows_n - 1))
    place = crow[...] * col_tiles + ccol[...]
    grid = (dests, amount)
    i = lax.broadcasted_iota(jnp.int32, grid, 1)
    here = lax.broadcasted_iota(jnp.int32, grid, 0) == address
    wide = (fronts, rows_n, 128)

    def spread(column):
        return jnp.broadcast_to(column, (dests, 128)).reshape(wide)

    first = jnp.min(jnp.where(here, i, amount), axis=1, keepdims=True)
    last = jnp.max(jnp.where(here, i, -1), axis=1, keepdims=True)
    place1 = jnp.sum(jnp.where(i == first, place, 0), axis=1, keepdims=True)
    place2 = jnp.sum(jnp.where(i == last, place, 0), axis=1, keepdims=True)
    place1 = spread(jnp.where(first < amount, place1, empty))
    pick1 = spread(jnp.where(first < amount, first, 0))
    twice = spread(jnp.where(last > first, 1, 0))
    place2, last = spread(place2), spread(last)
    lane = lax.broadcasted_iota(jnp.int32, wide, 2)
    r = lax.broadcasted_iota(jnp.int32, wide, 1)
    rank = jnp.zeros(wide, jnp.int32)
    for q in range(rows_n - 1):
        rank = rank + jnp.where(r > q, twice[:, q : q + 1, :], 0)
    few = jnp.where((rank == lane) & (lane < FEW), twice, 0)
    firsts = lane - 8 == r
    left = jnp.where(rank >= FEW, twice, 0)

    def down(value):
        return jnp.sum(value, axis=1, keepdims=True)

    row_lane = lax.broadcasted_iota(jnp.int32, (fronts, 1, 128), 2)
    over = jnp.sum(down(left), axis=0, keepdims=True)
    code = down(few * (r * empty + place2)) + down(jnp.where(firsts, place1, 0))
    code = jnp.where((row_lane < FEW) & (down(few) == 0), rows_n * empty, code)
    codes[...] = jnp.where(row_lane == FEW, over, code)
    picks[...] = down(few * last) + down(jnp.where(firsts, pick1, 0))
    idx3[...] = (left * last).reshape(dests, 128)
    place3[...] = jnp.where(left > 0, place2, empty).reshape(dests, 128)


def remote(src, dst, ssem, rsem, dev):
    return pltpu.make_async_remote_copy(src, dst, ssem, rsem, device_id=dev, device_id_type=MESH)


def level_kernel(fronts, rows_n, col_tiles, target, crow, ccol, owner, live, tiles_hbm, fown, wown_hbm, update,
                 inc, xin, places, over, base, panel, idx3, place3,
                 tiles, send, xsend, send2, in2, codes, picks, incode, pick_s, code_s,
                 fownv, fother, fcols, wown, wother, old, own_panel, half_panel, xcodes, ycodes,
                 ssem, rsem, xssem, xrsem, cssem, crsem, yssem, yrsem, ts, tr, cs, cr, ys, yr, xs, xr, ks, kr, ws, wr, wks, wkr, lsem):
    dests = fronts * rows_n
    empty = 4 * col_tiles
    front, row, col = lax.axis_index("front"), lax.axis_index("row"), lax.axis_index("col")
    me = front * rows_n + row
    x, k = row // 2, row % 2
    place_bits = empty.bit_length() - 1
    j = (x + 4 - 2 * col) % 4
    step_rows = fown.shape[0] // CHUNKS

    def at_j(place):
        return (front, ((place + 2 * col) % 4) * 2 + k, col)

    here = (front, row, col)
    mate = (front, x * 2 + 1 - k, col)
    across = (front, row, 1 - col)

    def part(i):
        return pl.ds(i * step_rows, step_rows)

    def load(n, src, dst):
        return pltpu.make_async_copy(src, dst, lsem.at[n])

    loads = [load(0, tiles_hbm, tiles), load(1, fown, fownv), load(2, wown_hbm, wown), load(3, update, old)]

    @pl.loop(0, CHUNKS)
    def _(i):
        remote(fown.at[part(i)], fother.at[part(i)], ys, yr.at[i], across).start()

    def give(which, half, i, src, dev):
        b = 2 * which + k
        remote(src, fcols.at[b, half, part(i)], xs, xr.at[which, half, i], dev).start()

    def to_mate(which, half, i, src):
        b = 2 * which + k
        remote(src, fcols.at[b, half, part(i)], ks, kr.at[which], mate).start()

    def own_out(half, i, src):
        @pl.when(j == 0)
        def _():
            give(0, half, i, src, at_j(3))
            give(0, half, i, src, at_j(1))
            to_mate(0, half, i, src)

        @pl.when(j == 1)
        def _():
            give(1, half, i, src, at_j(2))
            give(1, half, i, src, at_j(0))
            to_mate(1, half, i, src)

    @pl.loop(0, CHUNKS)
    def _(i):
        own_out(col, i, fown.at[part(i)])

    w_rows = wother.shape[0] // 2
    w_mine = pl.ds(pl.multiple_of(k * w_rows, TILE), w_rows)
    remote(wown_hbm.at[w_mine], wother.at[w_mine], ws, wr, across).start()
    for c in loads:
        c.start()

    make_tables(fronts, rows_n, col_tiles, target, crow, ccol, owner, codes, picks, idx3, place3)
    table = load(4, picks, pick_s)
    table.start()
    table.wait()
    loads[0].wait()

    for t in range(FEW):
        in2[front * FEW + t] = tiles[pick_s[front, 0, t]]
    incode[front] = codes[front]

    @pl.loop(1, fronts)
    def _(s):
        f = jnp.bitwise_xor(front, (s * 7) % fronts)
        for t in range(FEW):
            send2[f * FEW + t] = tiles[pick_s[f, 0, t]]
        dev = (f, row, col)
        remote(send2.at[pl.ds(f * FEW, FEW)], in2.at[pl.ds(front * FEW, FEW)], ts, tr, dev).start()
        remote(codes.at[f], incode.at[front], cs, cr, dev).start()

    send[me] = tiles[pick_s[front, 0, 8 + row]]
    own = load(5, send.at[me], inc.at[me])
    own.start()

    def arrived(which, half, i):
        b = 2 * which + k
        remote(fcols.at[b, half, part(i)], fcols.at[b, half, part(i)], xs, xr.at[which, half, i], mate).wait_recv()

    def pass_on(which, half, i, dev):
        b = 2 * which + k
        src = fcols.at[b, half, part(i)]
        if dev is not None:
            give(which, half, i, src, dev)
        to_mate(which, half, i, src)

    def straight(n):
        p = jnp.bitwise_xor(me, (n * 37) % dests)
        f, r = p // rows_n, p % rows_n
        send[p] = tiles[pick_s[f, 0, 8 + r]]
        remote(send.at[p], inc.at[me], ssem, rsem, (f, r, col)).start()

    per = EARLY // (2 * CHUNKS)

    @pl.loop(0, 2 * CHUNKS + 1)
    def _(s):
        @pl.when(s < 2 * CHUNKS)
        def _():
            @pl.loop(0, per)
            def _(inner):
                n = s * per + inner

                @pl.when(n > 0)
                def _():
                    straight(n)

            late = s // CHUNKS
            half = (col + late) % 2
            i = s % CHUNKS

            @pl.when(late == 1)
            def _():
                remote(fown.at[part(i)], fother.at[part(i)], ys, yr.at[i], across).wait_recv()
                own_out(half, i, fother.at[part(i)])

            @pl.when(s == CHUNKS)
            def _():
                whalf = remote(wother.at[w_mine], wother.at[w_mine], wks, wr, mate)
                whalf.wait_recv()
                remote(wother.at[w_mine], wother.at[w_mine], wks, wkr, mate).start()

            @pl.when(j == 0)
            def _():
                arrived(1, half, i)
                pass_on(1, half, i, None)

            @pl.when(j == 1)
            def _():
                arrived(0, half, i)
                pass_on(0, half, i, None)

            @pl.when(j == 2)
            def _():
                arrived(1, half, i)
                pass_on(1, half, i, at_j(3))

            @pl.when(j == 3)
            def _():
                arrived(0, half, i)
                pass_on(0, half, i, at_j(2))

        @pl.when(s > 0)
        def _():
            half = (col + (s - 1) // CHUNKS) % 2
            i = (s - 1) % CHUNKS

            @pl.when(j == 2)
            def _():
                arrived(0, half, i)
                pass_on(0, half, i, None)

            @pl.when(j == 3)
            def _():
                arrived(1, half, i)
                pass_on(1, half, i, None)

    some = pl.ds(0, (fronts - 1) * FEW)
    both = remote(send2.at[some], in2.at[some], ts, tr, mate)
    both.wait_send()
    both.wait_recv()
    most = pl.ds(0, fronts - 1)
    got = remote(codes.at[most], incode.at[most], cs, cr, mate)
    got.wait_send()
    got.wait_recv()
    table = load(4, incode, code_s)
    table.start()
    table.wait()

    def pack_one(r, g):
        t = 0
        for q in range(1, FEW):
            t = jnp.where(lax.shift_right_logical(code_s[g, 0, q], place_bits) == r, q, t)
        xsend[r * fronts + g] = in2[g * FEW + t]

    @pl.loop(0, rows_n)
    def _(s):
        r = jnp.bitwise_xor(row, s)

        @pl.when(s > 0)
        def _():
            remote(incode, xcodes.at[row], cssem, crsem, (front, r, col)).start()

        remote(incode, ycodes.at[row], yssem, yrsem, (front, r, 1 - col)).start()

    then = (dests - EARLY) // (rows_n - 1)

    @pl.loop(1, rows_n)
    def _(s):
        r = jnp.bitwise_xor(row, s)

        @pl.loop(0, fronts)
        def _(g):
            pack_one(r, g)

        src = xsend.at[pl.ds(r * fronts, fronts)]
        remote(src, xin.at[pl.ds(row * fronts, fronts)], xssem, xrsem, (front, r, col)).start()

        @pl.loop(0, then)
        def _(q):
            straight(EARLY + (s - 1) * then + q)

    @pl.loop(0, fronts)
    def _(g):
        pack_one(row, g)

    mine = pl.ds(row * fronts, fronts)
    ownx = load(4, xsend.at[mine], xin.at[mine])
    ownx.start()
    xcodes[row] = incode[...]

    for which in range(2):
        b = 2 * which + 1 - k
        remote(fcols.at[b], fcols.at[b], ks, kr.at[which], mate).wait_recv()
    w_other = pl.ds(pl.multiple_of((1 - k) * w_rows, TILE), w_rows)
    remote(wother.at[w_other], wother.at[w_other], wks, wkr, mate).wait_recv()
    for c in loads[1:]:
        c.wait()

    @pl.when(j < 2)
    def _():
        b = 2 * j + k
        fcols[b, col] = fownv[...]
        fcols[b, 1 - col] = fother[...]

    schur_base(live, fownv, fother, fcols, wown, wother, old, own_panel, half_panel)
    results = [load(1, old, base), load(2, half_panel, panel)]
    for c in results:
        c.start()


    some = pl.ds(0, rows_n - 1)
    both = remote(xcodes.at[some], xcodes.at[some], cssem, crsem, here)
    both.wait_send()
    both.wait_recv()
    both = remote(ycodes, ycodes, yssem, yrsem, here)
    both.wait_send()
    both.wait_recv()
    lane = lax.broadcasted_iota(jnp.int32, (fronts, 1, 128), 2)
    slot = lax.broadcasted_iota(jnp.int32, (fronts, 1, 128), 0)
    left = jnp.zeros((fronts, 1, 128), jnp.int32)
    for r in range(rows_n):
        code = xcodes[r]
        left = left + code + ycodes[r]
        one = jnp.sum(jnp.where(lane == 8 + row, code, 0), axis=2, keepdims=True)
        match = (lane < FEW) & (lax.shift_right_logical(code, place_bits) == row)
        two = jnp.min(jnp.where(match, code & (empty - 1), empty), axis=2, keepdims=True)
        places[r] = jnp.sum(jnp.where(lane == slot, one, 0) + jnp.where(lane == slot + fronts, two, 0), axis=0)
    over[0] = jnp.sum(jnp.where(lane == FEW, left, 0))

    remote(fown, fother, ys, yr.at[0], across).wait_send()
    remote(wother.at[w_mine], wother.at[w_mine], ws, wr, across).wait_send()
    remote(wother.at[w_mine], wother.at[w_mine], wks, wkr, mate).wait_send()
    pairs = fcols.at[pl.ds(0, 2)]
    remote(pairs, pairs, ks, kr.at[0], mate).wait_send()

    @pl.when(j < 2)
    def _():
        remote(pairs, pairs, xs, kr.at[0], mate).wait_send()

    @pl.when(j >= 2)
    def _():
        remote(fcols.at[0], fcols.at[0], xs, kr.at[0], mate).wait_send()

    own.wait()
    ownx.wait()
    for c in results:
        c.wait()
    some = pl.ds(0, dests - 1)
    both = remote(send.at[some], inc.at[some], ssem, rsem, here)
    both.wait_send()
    both.wait_recv()
    some = pl.ds(0, (rows_n - 1) * fronts)
    both = remote(xsend.at[some], xin.at[some], xssem, xrsem, here)
    both.wait_send()
    both.wait_recv()


def further_kernel(fronts, rows_n, idx, lab, tiles, inc, inlab, send, ssem, rsem, lssem, lrsem, lsem):
    dests = fronts * rows_n
    front, row, col = lax.axis_index("front"), lax.axis_index("row"), lax.axis_index("col")
    me = front * rows_n + row
    send[me] = tiles[idx[me]]
    own = pltpu.make_async_copy(send.at[me], inc.at[me], lsem.at[0])
    own.start()
    ownlab = pltpu.make_async_copy(lab.at[me], inlab.at[me], lsem.at[1])
    ownlab.start()

    @pl.loop(1, dests)
    def _(n):
        p = jnp.bitwise_xor(me, (n * 37) % dests)
        dev = (p // rows_n, p % rows_n, col)
        send[p] = tiles[idx[p]]
        remote(send.at[p], inc.at[me], ssem, rsem, dev).start()
        remote(lab.at[p], inlab.at[me], lssem, lrsem, dev).start()

    own.wait()
    ownlab.wait()
    some = pl.ds(0, dests - 1)
    both = remote(send.at[some], inc.at[some], ssem, rsem, (front, row, col))
    both.wait_send()
    both.wait_recv()
    labs = remote(lab.at[some], inlab.at[some], lssem, lrsem, (front, row, col))
    labs.wait_send()
    labs.wait_recv()


def add_tile(out, place, col_tiles, tile):
    @pl.when(place < 4 * col_tiles)
    def _():
        r = pl.multiple_of((place // col_tiles) * TILE, TILE)
        c = pl.multiple_of((place % col_tiles) * TILE, TILE)
        out[pl.ds(r, TILE), pl.ds(c, TILE)] += tile[...].astype(jnp.float32)


def more_kernel(group, col_tiles, lab, base, tiles, out):
    step = pl.program_id(0)

    @pl.when(step == 0)
    def _():
        out[...] = base[...]

    @pl.loop(0, group)
    def _(i):
        add_tile(out, lab[step * group + i, 0, 0], col_tiles, tiles.at[i])


def finish_kernel(fronts, rows_n, col_tiles, places, live, base, first, second, panel, out, panel_out,
                  fbuf, sbuf, total, old, obuf, fsem, ssem, osem, psem, bsem):
    row, col = lax.axis_index("row"), lax.axis_index("col")
    bound = live[0] * TILE
    height, width = total.shape
    copy = pltpu.make_async_copy

    def tiles_of(r):
        part = pl.ds(r * fronts, fronts)
        return copy(first.at[part], fbuf.at[part], fsem.at[r]), copy(second.at[part], sbuf.at[part], ssem.at[r])

    for r in range(rows_n):
        for c in tiles_of(r):
            c.start()
    fill = copy(base, old, bsem)
    fill.start()
    copy(panel, panel_out, psem).start()
    total[...] = jnp.zeros_like(total)

    @pl.loop(0, rows_n)
    def _(s):
        for c in tiles_of(s):
            c.wait()
        for i in range(fronts):
            front = s * (fronts // rows_n) + i // rows_n
            add_tile(total, places[i % rows_n, 0, front], col_tiles, fbuf.at[s * fronts + i])
            add_tile(total, places[s, 0, fronts + i], col_tiles, sbuf.at[s * fronts + i])

    fill.wait()

    def rows_out(i):
        rows = pl.ds(pl.multiple_of(i * TILE, TILE), TILE)
        return copy(obuf.at[rows], out.at[rows], osem.at[i])

    @pl.loop(0, height // TILE)
    def _(i):
        rows = pl.ds(pl.multiple_of(i * TILE, TILE), TILE)
        row_ids = row * height + i * TILE + lax.broadcasted_iota(jnp.int32, (TILE, 1), 0)
        col_ids = col * width + lax.broadcasted_iota(jnp.int32, (1, width), 1)
        inside = (row_ids < bound) & (col_ids < bound)
        obuf[rows] = jnp.where(inside, old[rows] + total[rows], 0.0).astype(obuf.dtype)
        rows_out(i).start()

    @pl.loop(0, height // TILE)
    def _(i):
        rows_out(i).wait()

    copy(panel, panel_out, psem).wait()


def per_device(
    update_block,
    front_panel,
    inverse_factor,
    child_tiles,
    child_target,
    child_row,
    child_col,
    front_owner,
    live_tiles,
):
    rows_dev = update_block.shape[1]
    cols_dev = update_block.shape[2]
    fronts = lax.axis_size("front")
    rows_n = lax.axis_size("row")
    dests = fronts * rows_n
    col_tiles = cols_dev // TILE
    half = front_panel.shape[2]

    anyspace = pl.BlockSpec(memory_space=pl.ANY)
    hbm = pl.BlockSpec(memory_space=pltpu.HBM)
    smem = pl.BlockSpec(memory_space=pltpu.SMEM)
    vmem = pl.BlockSpec(memory_space=pltpu.VMEM)
    shape = jax.ShapeDtypeStruct
    tile_shape = (TILE, TILE)
    ints = lambda *s: shape(s, jnp.int32)
    params = pltpu.CompilerParams(has_side_effects=True, vmem_limit_bytes=40 << 20)

    block = (rows_dev, cols_dev)
    group = dests // rows_n
    inc_shape = shape((dests,) + tile_shape, jnp.bfloat16)
    rows_buf = lambda *n: pltpu.VMEM(n + (rows_dev, half), jnp.float32)
    tiles_buf = lambda n: pltpu.VMEM((n,) + tile_shape, jnp.bfloat16)
    table = lambda space: space((fronts, 1, 128), jnp.int32)
    amount = child_tiles.shape[0]
    first, second, places, over, base, panel_half, idx3, place3 = pl.pallas_call(
        functools.partial(level_kernel, fronts, rows_n, col_tiles),
        out_shape=(inc_shape, inc_shape, ints(rows_n, 1, 128), ints(1), shape(block, jnp.float32),
                   shape((rows_dev, half), jnp.float32), ints(dests, 128), ints(dests, 128)),
        in_specs=[vmem, vmem, vmem, smem, smem, anyspace, anyspace, anyspace, anyspace],
        out_specs=(hbm, hbm, vmem, smem, hbm, hbm, vmem, vmem),
        scratch_shapes=[
            tiles_buf(amount), tiles_buf(dests), tiles_buf(dests), tiles_buf(fronts * FEW), tiles_buf(fronts * FEW),
            table(pltpu.VMEM), table(pltpu.VMEM), table(pltpu.VMEM), table(pltpu.SMEM), table(pltpu.SMEM),
            rows_buf(), rows_buf(), rows_buf(4, 2),
            pltpu.VMEM((2 * half, half), jnp.float32), pltpu.VMEM((2 * half, half), jnp.float32),
            pltpu.VMEM(block, jnp.float32), pltpu.VMEM((rows_dev, 2 * half), jnp.float32), rows_buf(),
            pltpu.VMEM((rows_n, fronts, 1, 128), jnp.int32), pltpu.VMEM((rows_n, fronts, 1, 128), jnp.int32),
        ] + [DMA] * 13 + [DMA((CHUNKS,)), DMA, DMA((2, 2, CHUNKS)), DMA, DMA((2,))] + [DMA] * 4 + [DMA((6,))],
        compiler_params=pltpu.CompilerParams(has_side_effects=True, vmem_limit_bytes=58 << 20),
        cost_estimate=pl.CostEstimate(flops=0, bytes_accessed=300_000_000, transcendentals=0),
        name="level",
    )(child_target.reshape(1, amount), child_row.reshape(1, amount), child_col.reshape(1, amount), front_owner, live_tiles,
      child_tiles, front_panel[0], inverse_factor[0], update_block[0])

    whole = pl.BlockSpec(block, lambda i: (0, 0), pipeline_mode=pl.Buffered(1))
    tiles_spec = pl.BlockSpec((group,) + tile_shape, lambda i: (i, 0, 0))

    def further(value):
        labels = jnp.broadcast_to(place3[:, :1, None], (dests, 1, 128))
        tiles3, labels3 = pl.pallas_call(
            functools.partial(further_kernel, fronts, rows_n),
            out_shape=(inc_shape, ints(dests, 1, 128)),
            in_specs=[smem, anyspace, vmem],
            out_specs=(anyspace,) * 2,
            scratch_shapes=[tiles_buf(dests)] + [DMA] * 4 + [DMA((2,))],
            compiler_params=params,
            name="further",
        )(idx3[:, 0], labels, child_tiles)
        return pl.pallas_call(
            functools.partial(more_kernel, group, col_tiles),
            out_shape=shape(block, jnp.float32),
            grid=(rows_n,),
            in_specs=[smem, whole, tiles_spec],
            out_specs=pl.BlockSpec(block, lambda i: (0, 0)),
            compiler_params=pltpu.CompilerParams(vmem_limit_bytes=40 << 20),
            name="more",
        )(labels3, value, tiles3)

    base = lax.cond(over[0] > 0, further, lambda value: value, base)

    schur_out, panel_out = pl.pallas_call(
        functools.partial(finish_kernel, fronts, rows_n, col_tiles),
        out_shape=(shape(block, jnp.bfloat16), shape((rows_dev, half), jnp.float32)),
        in_specs=[smem, smem, hbm, hbm, hbm, vmem],
        out_specs=(hbm, hbm),
        scratch_shapes=[
            tiles_buf(dests), tiles_buf(dests), pltpu.VMEM(block, jnp.float32), pltpu.VMEM(block, jnp.float32),
            pltpu.VMEM(block, jnp.bfloat16),
            DMA((rows_n,)), DMA((rows_n,)), DMA((rows_dev // TILE,)), DMA, DMA,
        ],
        compiler_params=pltpu.CompilerParams(vmem_limit_bytes=58 << 20),
        name="finish",
    )(places, live_tiles, base, first, second, panel_half)
    return (schur_out[None], panel_out[None])


def solution(mesh):
    return jax.shard_map(
        per_device,
        mesh=mesh,
        in_specs=(
            P("front", "row", "col"),
            P("front", "row", "col"),
            P("front", None, "col"),
            P(("front", "row", "col"), None, None),
            P(("front", "row", "col"), None),
            P(("front", "row", "col")),
            P(("front", "row", "col")),
            P(),
            P("front"),
        ),
        out_specs=(P("front", "row", "col"), P("front", "row", "col")),
        check_vma=False,
    )
```
